256 devices in a mesh: comp: 16 (over z, core), blk: 16 (over x, y).
Axes of the slice: x: 4, y: 4, z: 8, core: 2. Of those that a mesh axis runs over, the one named last changes fastest.
Arguments:
- state_now: float32 [16, 6, 128, 32, 256], P('comp', None, 'blk'), may hold values from -5 to 5
- state_prev: float32 [16, 6, 128, 32, 256], P('comp', None, 'blk'), may hold values from -5 to 5
- viscosity: float32 [16, 128, 32, 256], P('comp', 'blk'), may hold values from 0.05 to 0.5
- jacobian: float32 [16, 3, 6, 6], P('comp'), may hold values from -0.4 to 0.4
- donor_cell: int32 [16, 16, 16, 2, 8, 128], P('comp', 'blk'), may hold values from 0 to 57343, as said below
- interp_weight: float32 [16, 16, 16, 2, 8, 128], P('comp', 'blk'), may hold values from 0 to 1
- recv_cell: int32 [16, 16, 16, 2, 128], P('comp', 'blk'), may hold values from 0 to 57343, as said below
- pair_tiles: int32 [16, 16, 16], P('blk'), may hold values from 0 to 2, as said below
Outputs:
- state_next: float32 [16, 6, 128, 32, 256], P('comp', None, 'blk')
The draws below stay inside these ranges and needn't reach their ends.
Inputs may be any that keep to these rules, and one draw needn't show every extreme that they name: `donor_cell`: the cells of one donor tile point are the eight corners of a cube of adjacent cells, corner k = 4 i + 2 j + l offset by (i, j, l). `recv_cell`: the receiving cells of one device are all different. `pair_tiles`: for each block index some destination component takes 2 tiles from every source component.
All inputs are finite; a program needn't handle non-finite values.
Results may differ from the reference program's by a relative error of at most 0.0003.
Values sent between devices are 32-bit elements; how exact they have to be, the bound alone decides.
No kernel may reach another device: no remote copies, remote signals or barrier semaphores. Data moves between devices by JAX's collectives and lax.ppermute only.
A program may use at most 128 MiB of HBM per device.

```python
import math
import jax
import jax.numpy as jnp
from jax import lax

NV = 6
CX = 8
CY = 32
CZ = 256
SLOT = 2
TILE = 128
SUBITERS = 2
COMPS = 16
BLKS = 16
NX = 128
CELLS = 65536


def draw_donor_cell(key, part):
    shape = (COMPS, BLKS, COMPS, SLOT, TILE)
    first = jax.random.randint(jax.random.fold_in(key, 11), shape, 0, CX - 2)
    second = jax.random.randint(jax.random.fold_in(key, 12), shape, 0, CY - 1)
    third = jax.random.randint(jax.random.fold_in(key, 13), shape, 0, CZ - 1)
    corners = []
    for corner in range(8):
        off_a = corner // 4
        off_b = corner // 2 % 2
        off_c = corner % 2
        corners.append(((first + off_a) * CY + (second + off_b)) * CZ + (third + off_c))
    return jnp.stack(corners, axis=4).astype(jnp.int32)


def draw_interp_weight(key, part):
    shape = (3, COMPS, BLKS, COMPS, SLOT, TILE)
    frac = jax.random.uniform(jax.random.fold_in(key, 22), shape, jnp.float32)
    corners = []
    for corner in range(8):
        off_a = corner // 4
        off_b = corner // 2 % 2
        off_c = corner % 2
        part_a = frac[0] if off_a == 1 else 1.0 - frac[0]
        part_b = frac[1] if off_b == 1 else 1.0 - frac[1]
        part_c = frac[2] if off_c == 1 else 1.0 - frac[2]
        corners.append(part_a * part_b * part_c)
    return jnp.stack(corners, axis=4).astype(jnp.float32)


def draw_recv_cell(key, part):
    keys = jax.random.split(jax.random.fold_in(key, 31), COMPS * BLKS)

    def one_device(single):
        return jax.random.permutation(single, (CX - 1) * CY * CZ)[:COMPS * SLOT * TILE]
    chosen = jax.vmap(one_device)(keys)
    return chosen.reshape(COMPS, BLKS, COMPS, SLOT, TILE).astype(jnp.int32)


def draw_pair_tiles(key, part):
    counts = jax.random.randint(jax.random.fold_in(key, 41), (BLKS, COMPS, COMPS), 0, SLOT + 1)
    column = jax.random.randint(jax.random.fold_in(key, 42), (BLKS,), 0, COMPS)
    full = jnp.arange(COMPS, dtype=jnp.int32)[None, None, :] == column[:, None, None]
    return jnp.where(full, SLOT, counts).astype(jnp.int32)


def block_scale(own_key, extent, cuts, smallest, high):
    gain = 1.0
    for axis_at, shards_of in cuts:
        heights = jax.random.uniform(jax.random.fold_in(jax.random.fold_in(own_key, 6), axis_at), (shards_of,), jnp.float32, smallest / len(cuts), high / len(cuts))
        gain = gain * jnp.repeat(jnp.exp(heights), extent[axis_at] // shards_of).reshape((-1,) + (1,) * (len(extent) - 1 - axis_at))
    return gain


def bell_draw(own_key, shape, deviation, limit, pieces=(), held_as=jnp.bfloat16):
    factor_of = block_scale(own_key, shape, pieces, -0.22, 0.18) if pieces else 1.0
    drawn = jax.random.normal(own_key, shape, jnp.float32) * deviation * factor_of
    return jnp.minimum(jnp.maximum(drawn, -limit), limit).astype(held_as)


def setup_inputs(seed: int = 0) -> dict:
    streams_of = jax.random.split(jax.random.key(seed), 9)
    return {
        "state_now": bell_draw(streams_of[0], (COMPS, NV, NX, CY, CZ), 1.0, 5.0, ((0, 16), (2, 16)), jnp.float32),
        "state_prev": bell_draw(streams_of[1], (COMPS, NV, NX, CY, CZ), 1.0, 5.0, ((0, 16), (2, 16)), jnp.float32),
        "viscosity": jnp.clip(jnp.exp(math.log(0.5) - 2.3025851 * jax.random.uniform(streams_of[2], (COMPS, NX, CY, CZ), jnp.float32) ** block_scale(streams_of[2], (COMPS, NX, CY, CZ), ((0, 16), (1, 16)), -0.2, 0.2)), 0.05, 0.5),
        "jacobian": bell_draw(streams_of[3], (COMPS, 3, NV, NV), 0.1, 0.4, ((0, 16),), jnp.float32),
        "donor_cell": draw_donor_cell(jax.random.fold_in(streams_of[8], 71), 0),
        "interp_weight": draw_interp_weight(jax.random.fold_in(streams_of[8], 71), 0),
        "recv_cell": draw_recv_cell(jax.random.fold_in(streams_of[8], 71), 0),
        "pair_tiles": draw_pair_tiles(jax.random.fold_in(streams_of[8], 71), 0),
    }


time_scale = 0.5
pseudo_diag = 2.5


def mix(jac_dim, field):
    return jnp.einsum('vw,wxyz->vxyz', jac_dim, field, precision=lax.Precision.HIGHEST)


def flux(padded, kappa, jac):
    centre = padded[:, 1:-1]
    along_x = (padded[:, 2:] - padded[:, :-2]) * 0.5
    spread = jnp.pad(centre, ((0, 0), (0, 0), (1, 1), (1, 1)))
    along_y = (spread[:, :, 2:, 1:-1] - spread[:, :, :-2, 1:-1]) * 0.5
    along_z = (spread[:, :, 1:-1, 2:] - spread[:, :, 1:-1, :-2]) * 0.5
    beside = padded[:, 2:] + padded[:, :-2] + spread[:, :, 2:, 1:-1] + spread[:, :, :-2, 1:-1]
    beside = beside + spread[:, :, 1:-1, 2:] + spread[:, :, 1:-1, :-2]
    convect = mix(jac[0], along_x) + mix(jac[1], along_y) + mix(jac[2], along_z)
    return convect + kappa * (6.0 * centre - beside)


def relax(rstar, padded_step, kappa, diag, jac):
    centre = padded_step[:, 1:-1]
    return -(rstar + flux(padded_step, kappa, jac) - 6.0 * kappa * centre) / diag


def pad_rows(field):
    return jnp.pad(field, ((0, 0), (1, 1), (0, 0), (0, 0)))


def subiteration(items):
    state, now, prev, kappa, jac = items
    diag = pseudo_diag + 6.0 * kappa
    rstar = time_scale * (3.0 * state - 4.0 * now + prev) + flux(pad_rows(state), kappa, jac)
    first = -rstar / diag
    second = relax(rstar, pad_rows(first), kappa, diag, jac)
    third = relax(rstar, pad_rows(second), kappa, diag, jac)
    return state + third


def fringe(state, donor_cell, interp_weight, recv_cell, pair_tiles):
    comps = state.shape[0]
    nvar = state.shape[1]
    flat = state.reshape(comps, nvar, BLKS, CELLS).transpose(2, 0, 1, 3)
    donors = donor_cell.transpose(1, 0, 2, 3, 4, 5)
    weights = interp_weight.transpose(1, 0, 2, 3, 4, 5)
    cells_all = recv_cell.transpose(1, 0, 2, 3, 4)

    def one_block(items):
        blocks, donor_b, weight_b, cell_b, live_b = items

        def pick(block, index):
            return block[:, index.reshape(-1)]

        values = jax.vmap(pick)(blocks, donor_b).reshape(comps, nvar, comps, SLOT, 8, TILE)
        interp = jnp.einsum('caskp,avcskp->cvasp', weight_b, values, precision=lax.Precision.HIGHEST)

        def place(block, cells, incoming, live):
            index = cells.reshape(-1)
            keep = jnp.arange(SLOT, dtype=jnp.int32)[None, :] < live[:, None]
            keep = jnp.broadcast_to(keep[:, :, None], (comps, SLOT, TILE)).reshape(-1)
            old = block[:, index]
            return block.at[:, index].set(jnp.where(keep[None, :], incoming.reshape(nvar, -1), old))

        return jax.vmap(place)(blocks, cell_b, interp, live_b.T)

    result = lax.map(one_block, (flat, donors, weights, cells_all, pair_tiles))
    return result.transpose(1, 2, 0, 3).reshape(state.shape)


def reference(state_now, state_prev, viscosity, jacobian, donor_cell, interp_weight, recv_cell, pair_tiles):
    state = state_now
    for sub in range(SUBITERS):
        state = lax.map(subiteration, (state, state_now, state_prev, viscosity, jacobian))
        state = fringe(state, donor_cell, interp_weight, recv_cell, pair_tiles)
    return state
```

```python
import functools

import jax
import jax.numpy as jnp
from jax import lax
from jax.experimental import pallas as pl
from jax.experimental.pallas import tpu as pltpu
from jax.sharding import PartitionSpec as P

F32 = jnp.float32
I32 = jnp.int32
NV, CX, CY, CZ = 6, 8, 32, 256
LANES = 128
TILES = 32
POINTS = TILES * LANES
NT = CY // 8
YGROUPS = 11
DONOR_ROWS = 2 * YGROUPS * CZ
RECV_GROUPS = 2 * (CX - 1)
RECV_ROWS = RECV_GROUPS * CZ
PSEUDO_DIAG = 2.5
VMEM = pl.BlockSpec(memory_space=pltpu.VMEM)
SMEM = pl.BlockSpec(memory_space=pltpu.SMEM)
HBM = pl.BlockSpec(memory_space=pltpu.HBM)
ANY = pl.BlockSpec(memory_space=pl.ANY)
PADY = CY + 16
HALF = CZ // 2


def sds(shape, dtype=F32):
    return jax.ShapeDtypeStruct(shape, dtype)


def field(rows, pad=PADY):
    return pltpu.VMEM((NV, rows, 2, pad, LANES), F32)


def call(body, name, outs, ins, out_specs, scratch=(), vmem_mb=12, cost_us=1.0):
    outs = jax.tree.map(
        lambda o, spec: pltpu.HBM(o.shape, o.dtype) if spec is HBM else o, outs, out_specs
    )
    kernel = pl.pallas_call(
        body,
        out_shape=outs,
        in_specs=ins,
        out_specs=out_specs,
        scratch_shapes=list(scratch),
        compiler_params=pltpu.CompilerParams(vmem_limit_bytes=vmem_mb << 20),
        cost_estimate=pl.CostEstimate(
            flops=0, transcendentals=0, bytes_accessed=int(cost_us * 3.0e6)
        ),
        name=name,
    )

    def run(*args):
        return kernel(*[
            pltpu.with_memory_space_constraint(a, pltpu.HBM) if spec is HBM else a
            for a, spec in zip(args, ins, strict=True)
        ])

    return run


class Copies:
    def __init__(self, sem):
        self.sem, self.list = sem, []

    def add(self, src, dst):
        c = pltpu.make_async_copy(src, dst, self.sem)
        c.start()
        self.list.append(c)

    def halves(self, src, dst, y0=8):
        n = len(src.shape) - 2
        for h in range(2):
            full = (slice(None),) * n
            self.add(
                src.at[full + (slice(None), pl.ds(LANES * h, LANES))],
                dst.at[full + (h, pl.ds(y0, CY), slice(None))],
            )

    def halves_out(self, src, dst, y0=8):
        n = len(dst.shape) - 2
        for h in range(2):
            full = (slice(None),) * n
            self.add(
                src.at[full + (h, pl.ds(y0, CY), slice(None))],
                dst.at[full + (slice(None), pl.ds(LANES * h, LANES))],
            )

    def wait(self):
        for c in self.list:
            c.wait()
        self.list = []


def clear_pads(f, first, last):
    zero = jnp.zeros((8, LANES), F32)

    @pl.loop(first, last)
    def _(x):
        for v in range(NV):
            for h in range(2):
                f[v, x, h, 0:8, :] = zero
                f[v, x, h, PADY - 8 : PADY, :] = zero


def tile_terms(f, x, t, jh, kap):
    lane = lax.broadcasted_iota(I32, (8, LANES), 1)
    y0 = pl.multiple_of(8 * t + 8, 8)
    acc = [[None, None] for _ in range(NV)]
    centres = []
    for w in range(NV):
        c = [f[w, x, h, pl.ds(y0, 8), :] for h in range(2)]
        down = [pltpu.roll(c[h], 1, 1) for h in range(2)]
        up = [pltpu.roll(c[h], LANES - 1, 1) for h in range(2)]
        zm = [jnp.where(lane == 0, 0.0, down[0]), jnp.where(lane == 0, down[0], down[1])]
        zp = [
            jnp.where(lane == LANES - 1, up[1], up[0]),
            jnp.where(lane == LANES - 1, 0.0, up[1]),
        ]
        for h in range(2):
            xm, xp = f[w, x - 1, h, pl.ds(y0, 8), :], f[w, x + 1, h, pl.ds(y0, 8), :]
            ym, yp = f[w, x, h, pl.ds(y0 - 1, 8), :], f[w, x, h, pl.ds(y0 + 1, 8), :]
            dx, dy, dz = xp - xm, yp - ym, zp[h] - zm[h]
            beside = (xp + xm) + (yp + ym) + (zp[h] + zm[h])
            for v in range(NV):
                term = jh[v * 6 + w] * dx + jh[36 + v * 6 + w] * dy + jh[72 + v * 6 + w] * dz
                if v == w:
                    term = term - kap[h] * beside
                acc[v][h] = term if acc[v][h] is None else acc[v][h] + term
        centres.append(c)
    return acc, centres


def kap_tile(kap, k, t):
    y0 = pl.multiple_of(8 * t, 8)
    both = [kap[k, h, pl.ds(y0, 8), :] for h in range(2)]
    return both, [-1.0 / (PSEUDO_DIAG + 6.0 * b) for b in both]


def each_tile(count, row_of, body):
    @pl.loop(0, count * (NT // 2))
    def _(n):
        i = n // (NT // 2)
        row = row_of(i)
        for u in range(2):
            body(i, row, 2 * (n % (NT // 2)) + u)


def start_row(f, at, kap, k, now, prev, n, t, jh, emit):
    kp, ninv = kap_tile(kap, k, t)
    acc, centres = tile_terms(f, at, t, jh, kp)
    y0 = pl.multiple_of(8 * t, 8)
    for v in range(NV):
        for h in range(2):
            past = prev[v, n, h, pl.ds(y0, 8), :] - 4.0 * now[v, n, h, pl.ds(y0, 8), :]
            c = centres[v][h]
            r = 0.5 * (3.0 * c + past) + acc[v][h] + (6.0 * kp[h]) * c
            emit(v, h, r, r * ninv[h])


def relax_row(f, at, rs, ra, kap, k, t, jh, emit):
    kp, ninv = kap_tile(kap, k, t)
    acc, _ = tile_terms(f, at, t, jh, kp)
    y0 = pl.multiple_of(8 * t, 8)
    for v in range(NV):
        for h in range(2):
            emit(v, h, (rs[v, ra, h, pl.ds(y0, 8), :] + acc[v][h]) * ninv[h])


def edge_rows(f, kap, now, prev, jh, ers, es1):
    def body(i, row, t):
        y0 = pl.multiple_of(8 * t, 8)

        def emit(v, h, r, s):
            ers[v, i, h, pl.ds(y0, 8), :] = r
            es1[v, i, h, pl.ds(y0, 8), :] = s

        start_row(f, row + 1, kap, i, now, prev, i, t, jh, emit)

    each_tile(4, lambda i: i + 4 * (i // 2), body)


def edge_load(c, now, prev, kap, nowb, prevb, kapb):
    for i, x in ((0, 0), (2, 6)):
        c.halves(now.at[:, pl.ds(x, 2)], nowb.at[:, pl.ds(i, 2)], 0)
        c.halves(prev.at[:, pl.ds(x, 2)], prevb.at[:, pl.ds(i, 2)], 0)
        c.halves(kap.at[pl.ds(x, 2)], kapb.at[pl.ds(i, 2)], 0)


def edge_send(c, f, kap, ers, es1, lo, hi, er):
    for i, msg, row in ((0, lo, 0), (3, hi, CX - 1)):
        c.halves_out(f.at[:, row + 1], msg.at[pl.ds(0, NV)])
        c.halves_out(ers.at[:, i], msg.at[pl.ds(NV, NV)], 0)
        c.halves_out(es1.at[:, 1 + i // 3], msg.at[pl.ds(2 * NV, NV)], 0)
        c.halves_out(kap.at[i], msg.at[3 * NV], 0)
    c.halves_out(ers.at[:, pl.ds(1, 2)], er, 0)


def edge_zero(f):
    @pl.loop(0, CY // 8)
    def _(t):
        for v in range(NV):
            for h in range(2):
                for x in (0, CX + 1):
                    f[v, x, h, pl.ds(pl.multiple_of(8 * t + 8, 8), 8), :] = jnp.zeros((8, LANES), F32)


EDGE_SCRATCH = (
    field(4, CY), field(4, CY), pltpu.VMEM((4, 2, CY, LANES), F32),
    field(4, CY), field(4, CY),
)


def edge_body(now, prev, kap, jh, lo, hi, er, f, nowb, prevb, kapb, ers, es1, sem):
    c = Copies(sem.at[0])
    for x in (0, 5):
        c.halves(now.at[:, pl.ds(x, 3)], f.at[:, pl.ds(x + 1, 3)])
    edge_load(c, now, prev, kap, nowb, prevb, kapb)
    clear_pads(f, 1, 4)
    clear_pads(f, 6, 9)
    edge_zero(f)
    c.wait()
    edge_rows(f, kapb, nowb, prevb, jh, ers, es1)
    edge_send(c, f, kapb, ers, es1, lo, hi, er)
    c.wait()


def inner_body(
    q, now, prev, kap, jh, lo, hi, rs_out, s1_out, s2_out, s3_out,
    f, nowb, prevb, kapb, rs, s1, s2, s3, sem,
):
    c = Copies(sem.at[0])
    c.halves(q.at[:, pl.ds(1, 6)], f)
    c.halves(now.at[:, pl.ds(2, 4)], nowb, 0)
    c.halves(prev.at[:, pl.ds(2, 4)], prevb, 0)
    c.halves(kap.at[pl.ds(2, 4)], kapb, 0)
    c.halves(lo.at[pl.ds(2 * NV, NV)], s1.at[:, 0])
    c.halves(hi.at[pl.ds(2 * NV, NV)], s1.at[:, 5])
    clear_pads(f, 1, 5)
    clear_pads(s1, 1, 5)
    clear_pads(s2, 1, 3)
    c.wait()

    def first(i, row, t):
        def emit(v, h, r, s):
            rs[v, i, h, pl.ds(pl.multiple_of(8 * t, 8), 8), :] = r
            s1[v, i + 1, h, pl.ds(pl.multiple_of(8 * t + 8, 8), 8), :] = s

        start_row(f, i + 1, kapb, i, nowb, prevb, i, t, jh, emit)

    each_tile(4, lambda i: i, first)
    for i in range(2):
        c.halves_out(rs.at[:, 3 * i], rs_out.at[:, i], 0)
        c.halves_out(s1.at[:, 3 * i + 1], s1_out.at[:, i])

    def second(i, row, t):
        def emit(v, h, val):
            s2[v, i, h, pl.ds(pl.multiple_of(8 * t + 8, 8), 8), :] = val

        relax_row(s1, i + 1, rs, i, kapb, i, t, jh, emit)

    each_tile(4, lambda i: i, second)
    c.halves_out(s2, s2_out)

    def third(i, row, t):
        def emit(v, h, val):
            s3[v, i, h, pl.ds(pl.multiple_of(8 * t, 8), 8), :] = val

        relax_row(s2, i + 1, rs, i + 1, kapb, i + 1, t, jh, emit)

    each_tile(2, lambda i: i, third)
    c.halves_out(s3, s3_out, 0)
    c.wait()


INNER_SCRATCH = (
    field(6), field(4, CY), field(4, CY), pltpu.VMEM((4, 2, CY, LANES), F32),
    field(4, CY), field(6), field(4), field(2, CY), pltpu.SemaphoreType.DMA((1,)),
)


def fix_rows(rse, s1e, far, kape, jh, lo_ok, hi_ok):
    def body(i, row, t):
        y0 = pl.multiple_of(8 * t, 8)
        sign = jnp.where(i % 2 == 0, 1.0, -1.0).astype(F32)
        scale = jnp.where(i == 0, lo_ok, jnp.where(i == 3, hi_ok, 1.0))
        kp, ninv = kap_tile(kape, row + 1, t)
        for h in range(2):
            side = [far[w, i, h, pl.ds(y0, 8), :] for w in range(NV)]
            turned = [side[w] * sign for w in range(NV)]
            for v in range(NV):
                r = rse[v, row + 1, h, pl.ds(y0, 8), :] - kp[h] * side[v]
                for w in range(NV):
                    r = r + jh[v * 6 + w] * turned[w]
                rse[v, row + 1, h, pl.ds(y0, 8), :] = r
                s1e[v, row + 2, h, pl.ds(pl.multiple_of(y0 + 8, 8), 8), :] = r * (ninv[h] * scale)

    each_tile(4, lambda i: i - 1 + 6 * (i // 2), body)


def finish_body(
    q, kap, jh, who, idx_in, pairs_in, own_lo, own_hi, got_lo, got_hi, w_in,
    er, rs_in, s1_in, s2_in, s3_in, qn, send,
    rse, s1e, s2e, kape, far, qb, s3, q8, tab, g, wb, idx, pairs, sem,
):
    lo_ok = jnp.where(who[1] > 0, 1.0, 0.0).astype(F32)
    hi_ok = jnp.where(who[1] < who[2] - 1, 1.0, 0.0).astype(F32)
    c = Copies(sem.at[0])
    c.halves(kap, kape.at[pl.ds(1, CX)], 0)
    c.halves(got_lo.at[3 * NV], kape.at[0], 0)
    c.halves(got_hi.at[3 * NV], kape.at[CX + 1], 0)
    for i, msg in ((0, own_lo), (1, got_lo), (2, got_hi), (3, own_hi)):
        c.halves(msg.at[pl.ds(0, NV)], far.at[:, i], 0)
    for x, msg in ((0, got_lo), (1, own_lo), (8, own_hi), (9, got_hi)):
        c.halves(msg.at[pl.ds(NV, NV)], rse.at[:, x], 0)
    for x, msg in ((0, got_lo), (3, own_lo), (8, own_hi), (11, got_hi)):
        c.halves(msg.at[pl.ds(2 * NV, NV)], s1e.at[:, x])
    for i, (r, s) in enumerate(((2, 4), (7, 7))):
        c.halves(er.at[:, i], rse.at[:, r], 0)
        c.halves(rs_in.at[:, i], rse.at[:, (3, 6)[i]], 0)
        c.halves(s1_in.at[:, i], s1e.at[:, s])
    c.halves(s2_in, s2e.at[:, pl.ds(3, 4)])
    d = Copies(sem.at[1])
    d.halves(q, qb, 0)
    d.halves(s3_in, s3, 0)
    e = Copies(sem.at[2])
    e.add(w_in, wb)
    e.add(idx_in, idx)
    e.add(pairs_in, pairs)
    clear_pads(s1e, 1, 4)
    clear_pads(s1e, 8, 11)
    clear_pads(s2e, 1, 4)
    clear_pads(s2e, 6, 9)
    c.wait()

    fix_rows(rse, s1e, far, kape, jh, lo_ok, hi_ok)

    def second(i, row, t):
        scale = jnp.where(i == 0, lo_ok, jnp.where(i == 5, hi_ok, 1.0))

        def emit(v, h, val):
            s2e[v, row + 1, h, pl.ds(pl.multiple_of(8 * t + 8, 8), 8), :] = val * scale

        relax_row(s1e, row + 2, rse, row + 1, kape, row + 1, t, jh, emit)

    each_tile(6, lambda i: i - 1 + 4 * (i // 3), second)
    d.wait()

    def put(row, v, h, t, val):
        qb[v, row, h, pl.ds(pl.multiple_of(8 * t, 8), 8), :] = val
        q8[row, h, pl.ds(64 * t + v, 8, stride=8), :] = val

    def third(i, row, t):
        def emit(v, h, val):
            put(row, v, h, t, qb[v, row, h, pl.ds(pl.multiple_of(8 * t, 8), 8), :] + val)

        relax_row(s2e, row + 1, rse, row + 1, kape, row + 1, t, jh, emit)

    each_tile(6, lambda i: i + 2 * (i // 3), third)

    def rest(i, row, t):
        y0 = pl.multiple_of(8 * t, 8)
        for v in range(NV):
            for h in range(2):
                put(row, v, h, t, qb[v, row, h, pl.ds(y0, 8), :] + s3[v, i, h, pl.ds(y0, 8), :])

    each_tile(2, lambda i: i + 3, rest)
    d.halves_out(qb, qn, 0)
    gather_points(idx, pairs, who[0], wb, e, send, q8, tab, g)
    d.wait()


FINISH_SCRATCH = (
    field(CX + 2, CY), field(CX + 4), field(CX + 2), pltpu.VMEM((CX + 2, 2, CY, LANES), F32),
    field(4, CY), field(CX, CY), field(2, CY),
    pltpu.VMEM((CX, 2, 8 * CY, LANES), F32),
    pltpu.VMEM((DONOR_ROWS + 8, LANES), F32),
    pltpu.VMEM((2 * POINTS, LANES), F32),
    pltpu.VMEM((2, POINTS, LANES), F32),
    pltpu.SMEM((TILES, LANES), I32),
    pltpu.SMEM((16, 16), I32),
    pltpu.SemaphoreType.DMA((3,)),
)


def gather_points(idx, pairs, me, wb, loads, send, q8, tab, g):
    @pl.loop(0, YGROUPS)
    def _(yg):
        first = pl.multiple_of(jnp.minimum(yg * 3, CY - 4) * 8, 8)
        for xg in range(2):
            for h in range(2):
                block = [q8[xg * 3 + xx, h, pl.ds(first, 32), :] for xx in range(4)]
                row = pl.multiple_of((xg * YGROUPS + yg) * CZ + h * LANES, LANES)
                tab[pl.ds(row, LANES), :] = jnp.concatenate(block, axis=0).T

    loads.wait()

    @pl.loop(0, TILES)
    def _(tile):
        @pl.when(tile % 2 < pairs[me, tile // 2])
        def _():
            @pl.loop(0, LANES // 16)
            def _(b):
                for u in range(16):
                    row = idx[tile, b * 16 + u]
                    at = pl.multiple_of(tile * 256 + b * 32, 32) + 2 * u
                    g[pl.ds(at, 2), :] = tab[pl.ds(row, 2), :]

    @pl.loop(0, TILES // 4)
    def _(n):
        for u in range(4):
            o = pl.multiple_of(n * 4 * LANES + u * LANES, LANES)
            here = g[pl.ds(o * 2, LANES, stride=2), :] * wb[0, pl.ds(o, LANES), :]
            here = here + g[pl.ds(o * 2 + 1, LANES, stride=2), :] * wb[1, pl.ds(o, LANES), :]
            turned = here.T
            parts = [turned[8 * k : 8 * k + 8] for k in range(16)]
            while len(parts) > 1:
                parts = [a + b for a, b in zip(parts[::2], parts[1::2])]
            send[2 * n + u // 2, u % 2] = parts[0]


def setup_body(
    donor_in, recv_in, pairs_in, who, held_in, didx_out, ridx_out, rlane_out, w_out,
    donor, recv, pairs, held, didx, dpos, ridx, rlane, w, sem,
):
    c = Copies(sem.at[0])
    c.add(donor_in, donor)
    c.add(recv_in, recv)
    c.add(pairs_in, pairs)
    d = Copies(sem.at[1])
    d.add(held_in, held)
    c.wait()
    me = who[0]
    for s in range(16):
        live = pairs[s, me]
        for t in range(2):
            i = 2 * s + t
            cell = donor[s, t, 0:1, :]
            x, y, z = cell >> 13, (cell >> 8) & (CY - 1), cell & (CZ - 1)
            xg = jnp.where(x >= 3, 1, 0)
            yg = (y * 11) >> 5
            didx[i : i + 1, :] = (xg * YGROUPS + yg) * CZ + z
            dpos[i : i + 1, :] = (x - 3 * xg) * 4 + (y - jnp.minimum(yg * 3, CY - 4))
            cell = recv[s, t : t + 1, :]
            x, y, z = cell >> 13, (cell >> 8) & (CY - 1), cell & (CZ - 1)
            row = (2 * x + (y >> 4)) * CZ + z
            ridx[i : i + 1, :] = jnp.where(t < live, row, RECV_ROWS)
            rlane[i : i + 1, :] = y & 15
    c.add(didx, didx_out)
    c.add(ridx, ridx_out)
    c.add(rlane, rlane_out)
    d.wait()

    @pl.loop(0, TILES // 2)
    def _(n):
        for u in range(2):
            kpos = lax.broadcasted_iota(I32, (16, LANES), 0)
            base = jnp.broadcast_to(dpos[pl.ds(2 * n + u, 1), :], (16, LANES))
            o = pl.multiple_of(n * 2 * LANES + u * LANES, LANES)
            for l in range(2):
                grid = jnp.zeros((16, LANES), F32)
                for i in range(2):
                    for j in range(2):
                        k = 4 * i + 2 * j + l
                        row = jnp.broadcast_to(held[n, u, k : k + 1, :], (16, LANES))
                        grid = jnp.where(kpos == base + (4 * i + j), row, grid)
                wide = [jnp.broadcast_to(grid[k : k + 1], (8, LANES)) for k in range(16)]
                w[l, pl.ds(o, LANES), :] = jnp.concatenate(wide, axis=0).T

    d.add(w, w_out)
    c.wait()
    d.wait()


SETUP_SCRATCH = (
    pltpu.VMEM((16, 2, 8, LANES), I32),
    pltpu.VMEM((16, 2, LANES), I32),
    pltpu.SMEM((16, 16), I32),
    pltpu.VMEM((16, 2, 8, LANES), F32),
    pltpu.VMEM((TILES, LANES), I32),
    pltpu.VMEM((TILES, LANES), I32),
    pltpu.VMEM((TILES, LANES), I32),
    pltpu.VMEM((TILES, LANES), I32),
    pltpu.VMEM((2, POINTS, LANES), F32),
    pltpu.SemaphoreType.DMA((2,)),
)


def scatter_points(vals, ridx, rlane, qb, arrive, loads, f, y0, x0, vrep, u, ut):
    mark = lax.broadcasted_iota(I32, (8, LANES), 0) == NV
    lane = lax.broadcasted_iota(I32, (1, LANES), 1) >> 3

    @pl.loop(0, RECV_ROWS // LANES)
    def _(i):
        u[pl.ds(pl.multiple_of(i * LANES, LANES), LANES), :] = jnp.zeros((LANES, LANES), F32)

    @pl.loop(0, TILES // 4)
    def _(n):
        for k in range(4):
            v = jnp.where(mark, 1.0, vals[2 * n + k // 2, k % 2])
            rows = pl.ds(pl.multiple_of(n * 4 * LANES + k * LANES, LANES), LANES)
            vrep[rows, :] = jnp.concatenate([v] * 16, axis=0).T

    loads.wait()

    @pl.loop(0, TILES)
    def _(tile):
        @pl.loop(0, LANES // 16)
        def _(b):
            for j in range(16):
                row = ridx[tile, b * 16 + j]
                k = rlane[tile, b * 16 + j]
                at = pl.multiple_of(tile * LANES + b * 16, 16) + j
                pltpu.store(u.at[pl.ds(row, 1), :], vrep[pl.ds(at, 1), :], mask=lane == k)

    @pl.loop(0, CX - 1)
    def _(x):
        for yh in range(2):
            for h in range(2):
                row = pl.multiple_of((2 * x + yh) * CZ + h * LANES, LANES)
                ut[2 * x + yh, h] = u[pl.ds(row, LANES), :].T

    arrive.wait()

    @pl.loop(0, CX - 1)
    def _(x):
        for yh in range(2):
            for h in range(2):
                for t in range(2):
                    part = ut.at[2 * x + yh, h]
                    hit = part[pl.ds(64 * t + NV, 8, stride=8), :] != 0.0
                    y = 16 * yh + 8 * t
                    for v in range(NV):
                        new = part[pl.ds(64 * t + v, 8, stride=8), :]
                        f[v, x + x0, h, y0 + y : y0 + y + 8, :] = jnp.where(
                            hit, new, qb[v, x, h, y : y + 8, :]
                        )


def scatter_body(q, vals, ridx_in, rlane_in, out, qb, vrep, u, ut, ridx, rlane, sem):
    c, e = Copies(sem.at[0]), Copies(sem.at[2])
    e.add(ridx_in, ridx)
    e.add(rlane_in, rlane)
    c.halves(q, qb, 0)
    scatter_points(vals, ridx, rlane, qb, c, e, qb, 0, 0, vrep, u, ut)
    c.halves_out(qb, out, 0)
    c.wait()


def scatter_edge_body(
    q, vals, ridx_in, rlane_in, now, prev, kap, jh, out, lo, hi, er,
    qb, vrep, u, ut, ridx, rlane, f, nowb, prevb, kapb, ers, es1, sem,
):
    c, e = Copies(sem.at[0]), Copies(sem.at[2])
    e.add(ridx_in, ridx)
    e.add(rlane_in, rlane)
    c.halves(q, qb, 0)
    d = Copies(sem.at[1])
    edge_load(d, now, prev, kap, nowb, prevb, kapb)
    clear_pads(f, 1, 4)
    clear_pads(f, 6, 9)
    edge_zero(f)
    scatter_points(vals, ridx, rlane, qb, c, e, f, 8, 1, vrep, u, ut)
    for v in range(NV):
        for h in range(2):
            f[v, CX, h, 8 : 8 + CY, :] = qb[v, CX - 1, h]
    c.halves_out(f.at[:, pl.ds(1, CX)], out)
    d.wait()
    edge_rows(f, kapb, nowb, prevb, jh, ers, es1)
    edge_send(d, f, kapb, ers, es1, lo, hi, er)
    d.wait()
    c.wait()


STATE = (NV, CX, CY, CZ)
SCATTER_SCRATCH = (
    field(CX, CY),
    pltpu.VMEM((POINTS, LANES), F32),
    pltpu.VMEM((RECV_ROWS + 8, LANES), F32),
    pltpu.VMEM((RECV_GROUPS, 2, LANES, LANES), F32),
    pltpu.SMEM((TILES, LANES), I32),
    pltpu.SMEM((TILES, LANES), I32),
)


def rows_of(n):
    return sds((NV, n, CY, CZ))


def shards(
    state_now, state_prev, viscosity, jacobian, donor_cell, interp_weight, recv_cell, pair_tiles
):
    now = state_now[0]
    prev = state_prev[0]
    kap = viscosity[0]
    jh = (jacobian[0] * 0.5).reshape(-1)
    count = lax.axis_size("blk")
    at = lax.axis_index("blk")
    me = lax.axis_index("comp")
    who = jnp.stack([me, at, jnp.int32(count)]).astype(I32)
    pairs = pair_tiles[0]
    forward = [(i, i + 1) for i in range(count - 1)]
    backward = [(b, a) for a, b in forward]

    messages = [sds((3 * NV + 1, CY, CZ))] * 2 + [rows_of(2)]

    idx_shape = sds((TILES, LANES), I32)
    sems = pltpu.SemaphoreType.DMA((3,))

    lo, hi, er = call(
        edge_body, "edge", messages, [HBM] * 3 + [SMEM], [HBM] * 3,
        scratch=(field(CX + 2),) + EDGE_SCRATCH + (sems,), cost_us=3.0,
    )(now, prev, kap, jh)
    state = now
    for sub in range(2):
        got_lo = lax.ppermute(hi, "blk", forward)
        got_hi = lax.ppermute(lo, "blk", backward)
        inner = call(
            inner_body, "inner", [rows_of(n) for n in (2, 2, 4, 2)],
            [HBM] * 4 + [SMEM] + [HBM] * 2, [HBM] * 4,
            scratch=INNER_SCRATCH, vmem_mb=14, cost_us=4.0,
        )(state, now, prev, kap, jh, lo, hi)
        if sub == 0:
            weights, _ = lax.optimization_barrier((interp_weight[0, 0], lo))
            held = lax.all_to_all(weights, "comp", split_axis=0, concat_axis=0, tiled=True)
            didx, ridx, rlane, wide = call(
                setup_body, "setup", [idx_shape] * 3 + [sds((2, POINTS, LANES))],
                [HBM] * 3 + [SMEM, ANY], [HBM] * 4, scratch=SETUP_SCRATCH, cost_us=4.0,
            )(donor_cell[0, 0], recv_cell[0, 0], pairs, who, held)
        relaxed, send = call(
            finish_body, "finish", [sds(STATE), sds((16, 2, 8, LANES))],
            [HBM, HBM, SMEM, SMEM] + [HBM] * 4 + [ANY] * 2 + [HBM] * 6, [HBM, VMEM],
            scratch=FINISH_SCRATCH, vmem_mb=30, cost_us=14.0,
        )(
            state, kap, jh, who, didx, pairs, lo, hi, got_lo, got_hi, wide,
            er, *inner,
        )
        arrived = lax.all_to_all(send, "comp", split_axis=0, concat_axis=0, tiled=True)
        if sub == 0:
            state, lo, hi, er = call(
                scatter_edge_body, "scatter_edge", [sds(STATE)] + messages,
                [HBM, VMEM, HBM, HBM, HBM, HBM, HBM, SMEM], [HBM] * 4,
                scratch=SCATTER_SCRATCH + (field(CX + 2),) + EDGE_SCRATCH + (sems,),
                vmem_mb=20, cost_us=12.0,
            )(relaxed, arrived, ridx, rlane, now, prev, kap, jh)
        else:
            state = call(
                scatter_body, "scatter", sds(STATE), [HBM, VMEM, HBM, HBM], HBM,
                scratch=SCATTER_SCRATCH + (sems,), vmem_mb=12, cost_us=10.0,
            )(relaxed, arrived, ridx, rlane)
    return state[None]


def solution(mesh):
    in_specs = (
        P("comp", None, "blk", None, None),
        P("comp", None, "blk", None, None),
        P("comp", "blk", None, None),
        P("comp", None, None, None),
        P("comp", "blk", None, None, None, None),
        P("comp", "blk", None, None, None, None),
        P("comp", "blk", None, None, None),
        P("blk", None, None),
    )
    out_specs = P("comp", None, "blk", None, None)
    return jax.shard_map(shards, mesh=mesh, in_specs=in_specs, out_specs=out_specs, check_vma=False)
```

```python
import functools

import jax
import jax.numpy as jnp
from jax import lax
from jax.experimental import pallas as pl
from jax.experimental.pallas import tpu as pltpu
from jax.sharding import PartitionSpec as P

F32 = jnp.float32
I32 = jnp.int32
NV, CX, CY, CZ = 6, 8, 32, 256
LANES = 128
TILES = 32
POINTS = TILES * LANES
NT = CY // 8
YGROUPS = 11
DONOR_ROWS = 2 * YGROUPS * CZ
RECV_GROUPS = 2 * (CX - 1)
RECV_ROWS = RECV_GROUPS * CZ
PSEUDO_DIAG = 2.5
VMEM = pl.BlockSpec(memory_space=pltpu.VMEM)
SMEM = pl.BlockSpec(memory_space=pltpu.SMEM)
HBM = pl.BlockSpec(memory_space=pltpu.HBM)
ANY = pl.BlockSpec(memory_space=pl.ANY)
PADY = CY + 16
HALF = CZ // 2


def sds(shape, dtype=F32):
    return jax.ShapeDtypeStruct(shape, dtype)


def field(rows, pad=PADY):
    return pltpu.VMEM((NV, rows, 2, pad, LANES), F32)


def call(body, name, outs, ins, out_specs, scratch=(), vmem_mb=12, cost_us=1.0):
    outs = jax.tree.map(
        lambda o, spec: pltpu.HBM(o.shape, o.dtype) if spec is HBM else o, outs, out_specs
    )
    kernel = pl.pallas_call(
        body,
        out_shape=outs,
        in_specs=ins,
        out_specs=out_specs,
        scratch_shapes=list(scratch),
        compiler_params=pltpu.CompilerParams(vmem_limit_bytes=vmem_mb << 20),
        cost_estimate=pl.CostEstimate(
            flops=0, transcendentals=0, bytes_accessed=int(cost_us * 3.0e6)
        ),
        name=name,
    )

    def run(*args):
        return kernel(*[
            pltpu.with_memory_space_constraint(a, pltpu.HBM) if spec is HBM else a
            for a, spec in zip(args, ins, strict=True)
        ])

    return run


class Copies:
    def __init__(self, sem):
        self.sem, self.list = sem, []

    def add(self, src, dst):
        c = pltpu.make_async_copy(src, dst, self.sem)
        c.start()
        self.list.append(c)

    def halves(self, src, dst, y0=8):
        n = len(src.shape) - 2
        for h in range(2):
            full = (slice(None),) * n
            self.add(
                src.at[full + (slice(None), pl.ds(LANES * h, LANES))],
                dst.at[full + (h, pl.ds(y0, CY), slice(None))],
            )

    def halves_out(self, src, dst, y0=8):
        n = len(dst.shape) - 2
        for h in range(2):
            full = (slice(None),) * n
            self.add(
                src.at[full + (h, pl.ds(y0, CY), slice(None))],
                dst.at[full + (slice(None), pl.ds(LANES * h, LANES))],
            )

    def wait(self):
        for c in self.list:
            c.wait()
        self.list = []


def clear_pads(f, first, last):
    zero = jnp.zeros((8, LANES), F32)

    @pl.loop(first, last)
    def _(x):
        for v in range(NV):
            for h in range(2):
                f[v, x, h, 0:8, :] = zero
                f[v, x, h, PADY - 8 : PADY, :] = zero


def tile_terms(f, x, t, jh, kap):
    lane = lax.broadcasted_iota(I32, (8, LANES), 1)
    y0 = pl.multiple_of(8 * t + 8, 8)
    acc = [[None, None] for _ in range(NV)]
    centres = []
    for w in range(NV):
        c = [f[w, x, h, pl.ds(y0, 8), :] for h in range(2)]
        down = [pltpu.roll(c[h], 1, 1) for h in range(2)]
        up = [pltpu.roll(c[h], LANES - 1, 1) for h in range(2)]
        zm = [jnp.where(lane == 0, 0.0, down[0]), jnp.where(lane == 0, down[0], down[1])]
        zp = [
            jnp.where(lane == LANES - 1, up[1], up[0]),
            jnp.where(lane == LANES - 1, 0.0, up[1]),
        ]
        for h in range(2):
            xm, xp = f[w, x - 1, h, pl.ds(y0, 8), :], f[w, x + 1, h, pl.ds(y0, 8), :]
            ym, yp = f[w, x, h, pl.ds(y0 - 1, 8), :], f[w, x, h, pl.ds(y0 + 1, 8), :]
            dx, dy, dz = xp - xm, yp - ym, zp[h] - zm[h]
            beside = (xp + xm) + (yp + ym) + (zp[h] + zm[h])
            for v in range(NV):
                term = jh[v * 6 + w] * dx + jh[36 + v * 6 + w] * dy + jh[72 + v * 6 + w] * dz
                if v == w:
                    term = term - kap[h] * beside
                acc[v][h] = term if acc[v][h] is None else acc[v][h] + term
        centres.append(c)
    return acc, centres


def kap_tile(kap, k, t):
    y0 = pl.multiple_of(8 * t, 8)
    both = [kap[k, h, pl.ds(y0, 8), :] for h in range(2)]
    return both, [-1.0 / (PSEUDO_DIAG + 6.0 * b) for b in both]


def each_tile(count, row_of, body):
    @pl.loop(0, count * (NT // 2))
    def _(n):
        i = n // (NT // 2)
        row = row_of(i)
        for u in range(2):
            body(i, row, 2 * (n % (NT // 2)) + u)


def start_row(f, at, kap, k, now, prev, n, t, jh, emit):
    kp, ninv = kap_tile(kap, k, t)
    acc, centres = tile_terms(f, at, t, jh, kp)
    y0 = pl.multiple_of(8 * t, 8)
    for v in range(NV):
        for h in range(2):
            past = prev[v, n, h, pl.ds(y0, 8), :] - 4.0 * now[v, n, h, pl.ds(y0, 8), :]
            c = centres[v][h]
            r = 0.5 * (3.0 * c + past) + acc[v][h] + (6.0 * kp[h]) * c
            emit(v, h, r, r * ninv[h])


def relax_row(f, at, rs, ra, kap, k, t, jh, emit):
    kp, ninv = kap_tile(kap, k, t)
    acc, _ = tile_terms(f, at, t, jh, kp)
    y0 = pl.multiple_of(8 * t, 8)
    for v in range(NV):
        for h in range(2):
            emit(v, h, (rs[v, ra, h, pl.ds(y0, 8), :] + acc[v][h]) * ninv[h])


def edge_rows(f, kap, now, prev, jh, ers, es1):
    def body(i, row, t):
        y0 = pl.multiple_of(8 * t, 8)

        def emit(v, h, r, s):
            ers[v, i, h, pl.ds(y0, 8), :] = r
            es1[v, i, h, pl.ds(y0, 8), :] = s

        start_row(f, row + 1, kap, i, now, prev, i, t, jh, emit)

    each_tile(4, lambda i: i + 4 * (i // 2), body)


def edge_load(c, now, prev, kap, nowb, prevb, kapb):
    for i, x in ((0, 0), (2, 6)):
        c.halves(now.at[:, pl.ds(x, 2)], nowb.at[:, pl.ds(i, 2)], 0)
        c.halves(prev.at[:, pl.ds(x, 2)], prevb.at[:, pl.ds(i, 2)], 0)
        c.halves(kap.at[pl.ds(x, 2)], kapb.at[pl.ds(i, 2)], 0)


def edge_send(c, f, kap, ers, es1, lo, hi, er):
    for i, msg, row in ((0, lo, 0), (3, hi, CX - 1)):
        c.halves_out(f.at[:, row + 1], msg.at[pl.ds(0, NV)])
        c.halves_out(ers.at[:, i], msg.at[pl.ds(NV, NV)], 0)
        c.halves_out(es1.at[:, 1 + i // 3], msg.at[pl.ds(2 * NV, NV)], 0)
        c.halves_out(kap.at[i], msg.at[3 * NV], 0)
    c.halves_out(ers.at[:, pl.ds(1, 2)], er, 0)


def edge_zero(f):
    @pl.loop(0, CY // 8)
    def _(t):
        for v in range(NV):
            for h in range(2):
                for x in (0, CX + 1):
                    f[v, x, h, pl.ds(pl.multiple_of(8 * t + 8, 8), 8), :] = jnp.zeros((8, LANES), F32)


EDGE_SCRATCH = (
    field(4, CY), field(4, CY), pltpu.VMEM((4, 2, CY, LANES), F32),
    field(4, CY), field(4, CY),
)


def edge_body(now, prev, kap, jh, lo, hi, er, f, nowb, prevb, kapb, ers, es1, sem):
    c = Copies(sem.at[0])
    for x in (0, 5):
        c.halves(now.at[:, pl.ds(x, 3)], f.at[:, pl.ds(x + 1, 3)])
    edge_load(c, now, prev, kap, nowb, prevb, kapb)
    clear_pads(f, 1, 4)
    clear_pads(f, 6, 9)
    edge_zero(f)
    c.wait()
    edge_rows(f, kapb, nowb, prevb, jh, ers, es1)
    edge_send(c, f, kapb, ers, es1, lo, hi, er)
    c.wait()


def inner_body(
    q, now, prev, kap, jh, lo, hi, rs_out, s1_out, s2_out, s3_out,
    f, nowb, prevb, kapb, rs, s1, s2, s3, sem,
):
    c = Copies(sem.at[0])
    c.halves(q.at[:, pl.ds(1, 6)], f)
    c.halves(now.at[:, pl.ds(2, 4)], nowb, 0)
    c.halves(prev.at[:, pl.ds(2, 4)], prevb, 0)
    c.halves(kap.at[pl.ds(2, 4)], kapb, 0)
    c.halves(lo.at[pl.ds(2 * NV, NV)], s1.at[:, 0])
    c.halves(hi.at[pl.ds(2 * NV, NV)], s1.at[:, 5])
    clear_pads(f, 1, 5)
    clear_pads(s1, 1, 5)
    clear_pads(s2, 1, 3)
    c.wait()

    def first(i, row, t):
        def emit(v, h, r, s):
            rs[v, i, h, pl.ds(pl.multiple_of(8 * t, 8), 8), :] = r
            s1[v, i + 1, h, pl.ds(pl.multiple_of(8 * t + 8, 8), 8), :] = s

        start_row(f, i + 1, kapb, i, nowb, prevb, i, t, jh, emit)

    each_tile(4, lambda i: i, first)
    for i in range(2):
        c.halves_out(rs.at[:, 3 * i], rs_out.at[:, i], 0)
        c.halves_out(s1.at[:, 3 * i + 1], s1_out.at[:, i])

    def second(i, row, t):
        def emit(v, h, val):
            s2[v, i, h, pl.ds(pl.multiple_of(8 * t + 8, 8), 8), :] = val

        relax_row(s1, i + 1, rs, i, kapb, i, t, jh, emit)

    each_tile(4, lambda i: i, second)
    c.halves_out(s2, s2_out)

    def third(i, row, t):
        def emit(v, h, val):
            s3[v, i, h, pl.ds(pl.multiple_of(8 * t, 8), 8), :] = val

        relax_row(s2, i + 1, rs, i + 1, kapb, i + 1, t, jh, emit)

    each_tile(2, lambda i: i, third)
    c.halves_out(s3, s3_out, 0)
    c.wait()


INNER_SCRATCH = (
    field(6), field(4, CY), field(4, CY), pltpu.VMEM((4, 2, CY, LANES), F32),
    field(4, CY), field(6), field(4), field(2, CY), pltpu.SemaphoreType.DMA((1,)),
)


def fix_rows(rse, s1e, far, kape, jh, lo_ok, hi_ok):
    def body(i, row, t):
        y0 = pl.multiple_of(8 * t, 8)
        sign = jnp.where(i % 2 == 0, 1.0, -1.0).astype(F32)
        scale = jnp.where(i == 0, lo_ok, jnp.where(i == 3, hi_ok, 1.0))
        kp, ninv = kap_tile(kape, row + 1, t)
        for h in range(2):
            side = [far[w, i, h, pl.ds(y0, 8), :] for w in range(NV)]
            turned = [side[w] * sign for w in range(NV)]
            for v in range(NV):
                r = rse[v, row + 1, h, pl.ds(y0, 8), :] - kp[h] * side[v]
                for w in range(NV):
                    r = r + jh[v * 6 + w] * turned[w]
                rse[v, row + 1, h, pl.ds(y0, 8), :] = r
                s1e[v, row + 2, h, pl.ds(pl.multiple_of(y0 + 8, 8), 8), :] = r * (ninv[h] * scale)

    each_tile(4, lambda i: i - 1 + 6 * (i // 2), body)


def finish_body(
    q, kap, jh, who, idx_in, pairs_in, own_lo, own_hi, got_lo, got_hi, w_in,
    er, rs_in, s1_in, s2_in, s3_in, qn, send,
    rse, s1e, s2e, kape, far, qb, s3, q8, tab, g, wb, idx, pairs, sem,
):
    lo_ok = jnp.where(who[1] > 0, 1.0, 0.0).astype(F32)
    hi_ok = jnp.where(who[1] < who[2] - 1, 1.0, 0.0).astype(F32)
    c = Copies(sem.at[0])
    c.halves(kap, kape.at[pl.ds(1, CX)], 0)
    c.halves(got_lo.at[3 * NV], kape.at[0], 0)
    c.halves(got_hi.at[3 * NV], kape.at[CX + 1], 0)
    for i, msg in ((0, own_lo), (1, got_lo), (2, got_hi), (3, own_hi)):
        c.halves(msg.at[pl.ds(0, NV)], far.at[:, i], 0)
    for x, msg in ((0, got_lo), (1, own_lo), (8, own_hi), (9, got_hi)):
        c.halves(msg.at[pl.ds(NV, NV)], rse.at[:, x], 0)
    for x, msg in ((0, got_lo), (3, own_lo), (8, own_hi), (11, got_hi)):
        c.halves(msg.at[pl.ds(2 * NV, NV)], s1e.at[:, x])
    for i, (r, s) in enumerate(((2, 4), (7, 7))):
        c.halves(er.at[:, i], rse.at[:, r], 0)
        c.halves(rs_in.at[:, i], rse.at[:, (3, 6)[i]], 0)
        c.halves(s1_in.at[:, i], s1e.at[:, s])
    c.halves(s2_in, s2e.at[:, pl.ds(3, 4)])
    d = Copies(sem.at[1])
    d.halves(q, qb, 0)
    d.halves(s3_in, s3, 0)
    e = Copies(sem.at[2])
    e.add(w_in, wb)
    e.add(idx_in, idx)
    e.add(pairs_in, pairs)
    clear_pads(s1e, 1, 4)
    clear_pads(s1e, 8, 11)
    clear_pads(s2e, 1, 4)
    clear_pads(s2e, 6, 9)
    c.wait()

    fix_rows(rse, s1e, far, kape, jh, lo_ok, hi_ok)

    def second(i, row, t):
        scale = jnp.where(i == 0, lo_ok, jnp.where(i == 5, hi_ok, 1.0))

        def emit(v, h, val):
            s2e[v, row + 1, h, pl.ds(pl.multiple_of(8 * t + 8, 8), 8), :] = val * scale

        relax_row(s1e, row + 2, rse, row + 1, kape, row + 1, t, jh, emit)

    each_tile(6, lambda i: i - 1 + 4 * (i // 3), second)
    d.wait()

    def put(row, v, h, t, val):
        qb[v, row, h, pl.ds(pl.multiple_of(8 * t, 8), 8), :] = val
        q8[row, h, pl.ds(64 * t + v, 8, stride=8), :] = val

    def third(i, row, t):
        def emit(v, h, val):
            put(row, v, h, t, qb[v, row, h, pl.ds(pl.multiple_of(8 * t, 8), 8), :] + val)

        relax_row(s2e, row + 1, rse, row + 1, kape, row + 1, t, jh, emit)

    each_tile(6, lambda i: i + 2 * (i // 3), third)

    def rest(i, row, t):
        y0 = pl.multiple_of(8 * t, 8)
        for v in range(NV):
            for h in range(2):
                put(row, v, h, t, qb[v, row, h, pl.ds(y0, 8), :] + s3[v, i, h, pl.ds(y0, 8), :])

    each_tile(2, lambda i: i + 3, rest)
    d.halves_out(qb, qn, 0)
    gather_points(idx, pairs, who[0], wb, e, send, q8, tab, g)
    d.wait()


FINISH_SCRATCH = (
    field(CX + 2, CY), field(CX + 4), field(CX + 2), pltpu.VMEM((CX + 2, 2, CY, LANES), F32),
    field(4, CY), field(CX, CY), field(2, CY),
    pltpu.VMEM((CX, 2, 8 * CY, LANES), F32),
    pltpu.VMEM((DONOR_ROWS + 8, LANES), F32),
    pltpu.VMEM((2 * POINTS, LANES), F32),
    pltpu.VMEM((2, POINTS, LANES), F32),
    pltpu.SMEM((POINTS,), I32),
    pltpu.SMEM((16, 16), I32),
    pltpu.SemaphoreType.DMA((3,)),
)


def gather_points(idx, pairs, me, wb, loads, send, q8, tab, g):
    @pl.loop(0, YGROUPS)
    def _(yg):
        first = pl.multiple_of(jnp.minimum(yg * 3, CY - 4) * 8, 8)
        for xg in range(2):
            for h in range(2):
                block = [q8[xg * 3 + xx, h, pl.ds(first, 32), :] for xx in range(4)]
                row = pl.multiple_of((xg * YGROUPS + yg) * CZ + h * LANES, LANES)
                tab[pl.ds(row, LANES), :] = jnp.concatenate(block, axis=0).T

    loads.wait()

    @pl.loop(0, TILES)
    def _(tile):
        @pl.when(tile % 2 < pairs[me, tile // 2])
        def _():
            @pl.loop(0, LANES // 64)
            def _(b):
                for u in range(64):
                    row = idx[pl.multiple_of(tile * LANES + b * 64, 64) + u]
                    at = pl.multiple_of(tile * 256 + b * 128, 128) + 2 * u
                    g[pl.ds(at, 2), :] = tab[pl.ds(row, 2), :]

    @pl.loop(0, TILES // 8)
    def _(n):
        for u in range(8):
            o = pl.multiple_of(n * 8 * LANES + u * LANES, LANES)
            here = g[pl.ds(o * 2, LANES, stride=2), :] * wb[0, pl.ds(o, LANES), :]
            here = here + g[pl.ds(o * 2 + 1, LANES, stride=2), :] * wb[1, pl.ds(o, LANES), :]
            turned = here.T
            parts = [turned[8 * k : 8 * k + 8] for k in range(16)]
            while len(parts) > 1:
                parts = [a + b for a, b in zip(parts[::2], parts[1::2])]
            send[4 * n + u // 2, u % 2] = parts[0]


def setup_body(
    donor_in, recv_in, pairs_in, who, held_in, didx_out, ridx_out, w_out,
    donor, recv, pairs, held, didx, dpos, ridx, w, sem,
):
    c = Copies(sem.at[0])
    c.add(donor_in, donor)
    c.add(recv_in, recv)
    c.add(pairs_in, pairs)
    d = Copies(sem.at[1])
    d.add(held_in, held)
    c.wait()
    me = who[0]
    for s in range(16):
        live = pairs[s, me]
        for t in range(2):
            i = 2 * s + t
            cell = donor[s, t, 0:1, :]
            x, y, z = cell >> 13, (cell >> 8) & (CY - 1), cell & (CZ - 1)
            xg = jnp.where(x >= 3, 1, 0)
            yg = (y * 11) >> 5
            didx[i : i + 1, :] = (xg * YGROUPS + yg) * CZ + z
            dpos[i : i + 1, :] = (x - 3 * xg) * 4 + (y - jnp.minimum(yg * 3, CY - 4))
            cell = recv[s, t : t + 1, :]
            x, y, z = cell >> 13, (cell >> 8) & (CY - 1), cell & (CZ - 1)
            row = (2 * x + (y >> 4)) * CZ + z
            row = jnp.where(t < live, row, RECV_ROWS)
            ridx[i : i + 1, :] = row * 16 + (y & 15)
    c.add(didx, didx_out)
    c.add(ridx, ridx_out)
    d.wait()

    @pl.loop(0, TILES // 4)
    def _(m):
        for n, u in ((2 * m, 0), (2 * m, 1), (2 * m + 1, 0), (2 * m + 1, 1)):
            kpos = lax.broadcasted_iota(I32, (16, LANES), 0)
            base = jnp.broadcast_to(dpos[pl.ds(2 * n + u, 1), :], (16, LANES))
            o = pl.multiple_of(n * 2 * LANES + u * LANES, LANES)
            for l in range(2):
                grid = jnp.zeros((16, LANES), F32)
                for i in range(2):
                    for j in range(2):
                        k = 4 * i + 2 * j + l
                        row = jnp.broadcast_to(held[n, u, k : k + 1, :], (16, LANES))
                        grid = jnp.where(kpos == base + (4 * i + j), row, grid)
                wide = [jnp.broadcast_to(grid[k : k + 1], (8, LANES)) for k in range(16)]
                w[l, pl.ds(o, LANES), :] = jnp.concatenate(wide, axis=0).T

    d.add(w, w_out)
    c.wait()
    d.wait()


SETUP_SCRATCH = (
    pltpu.VMEM((16, 2, 8, LANES), I32),
    pltpu.VMEM((16, 2, LANES), I32),
    pltpu.SMEM((16, 16), I32),
    pltpu.VMEM((16, 2, 8, LANES), F32),
    pltpu.VMEM((TILES, LANES), I32),
    pltpu.VMEM((TILES, LANES), I32),
    pltpu.VMEM((TILES, LANES), I32),
    pltpu.VMEM((2, POINTS, LANES), F32),
    pltpu.SemaphoreType.DMA((2,)),
)


def scatter_points(vals, ridx, qb, arrive, loads, f, y0, x0, vrep, u, ut):
    mark = lax.broadcasted_iota(I32, (8, LANES), 0) == NV
    lane = lax.broadcasted_iota(I32, (1, LANES), 1) >> 3

    @pl.loop(0, RECV_ROWS // LANES)
    def _(i):
        u[pl.ds(pl.multiple_of(i * LANES, LANES), LANES), :] = jnp.zeros((LANES, LANES), F32)

    @pl.loop(0, TILES // 8)
    def _(n):
        for k in range(8):
            v = jnp.where(mark, 1.0, vals[4 * n + k // 2, k % 2])
            rows = pl.ds(pl.multiple_of(n * 8 * LANES + k * LANES, LANES), LANES)
            vrep[rows, :] = jnp.concatenate([v] * 16, axis=0).T

    loads.wait()

    @pl.loop(0, POINTS // 64)
    def _(b):
        for j in range(64):
            at = pl.multiple_of(b * 64, 64) + j
            word = ridx[at]
            mask = (jnp.full((1, LANES), word, I32) & 15) == lane
            pltpu.store(u.at[pl.ds(word >> 4, 1), :], vrep[pl.ds(at, 1), :], mask=mask)

    @pl.loop(0, CX - 1)
    def _(x):
        for yh in range(2):
            for h in range(2):
                row = pl.multiple_of((2 * x + yh) * CZ + h * LANES, LANES)
                ut[2 * x + yh, h] = u[pl.ds(row, LANES), :].T

    arrive.wait()

    @pl.loop(0, CX - 1)
    def _(x):
        for yh in range(2):
            for h in range(2):
                for t in range(2):
                    part = ut.at[2 * x + yh, h]
                    hit = part[pl.ds(64 * t + NV, 8, stride=8), :] != 0.0
                    y = 16 * yh + 8 * t
                    for v in range(NV):
                        new = part[pl.ds(64 * t + v, 8, stride=8), :]
                        f[v, x + x0, h, y0 + y : y0 + y + 8, :] = jnp.where(
                            hit, new, qb[v, x, h, y : y + 8, :]
                        )


def scatter_body(q, vals, ridx_in, out, qb, vrep, u, ut, ridx, sem):
    c, e = Copies(sem.at[0]), Copies(sem.at[2])
    e.add(ridx_in, ridx)
    c.halves(q, qb, 0)
    scatter_points(vals, ridx, qb, c, e, qb, 0, 0, vrep, u, ut)
    c.halves_out(qb, out, 0)
    c.wait()


def scatter_edge_body(
    q, vals, ridx_in, now, prev, kap, jh, out, lo, hi, er,
    qb, vrep, u, ut, ridx, f, nowb, prevb, kapb, ers, es1, sem,
):
    c, e = Copies(sem.at[0]), Copies(sem.at[2])
    e.add(ridx_in, ridx)
    c.halves(q, qb, 0)
    d = Copies(sem.at[1])
    edge_load(d, now, prev, kap, nowb, prevb, kapb)
    clear_pads(f, 1, 4)
    clear_pads(f, 6, 9)
    edge_zero(f)
    scatter_points(vals, ridx, qb, c, e, f, 8, 1, vrep, u, ut)
    for v in range(NV):
        for h in range(2):
            f[v, CX, h, 8 : 8 + CY, :] = qb[v, CX - 1, h]
    c.halves_out(f.at[:, pl.ds(1, CX)], out)
    d.wait()
    edge_rows(f, kapb, nowb, prevb, jh, ers, es1)
    edge_send(d, f, kapb, ers, es1, lo, hi, er)
    d.wait()
    c.wait()


STATE = (NV, CX, CY, CZ)
SCATTER_SCRATCH = (
    field(CX, CY),
    pltpu.VMEM((POINTS, LANES), F32),
    pltpu.VMEM((RECV_ROWS + 8, LANES), F32),
    pltpu.VMEM((RECV_GROUPS, 2, LANES, LANES), F32),
    pltpu.SMEM((POINTS,), I32),
)


def rows_of(n):
    return sds((NV, n, CY, CZ))


def shards(
    state_now, state_prev, viscosity, jacobian, donor_cell, interp_weight, recv_cell, pair_tiles
):
    now = state_now[0]
    prev = state_prev[0]
    kap = viscosity[0]
    jh = (jacobian[0] * 0.5).reshape(-1)
    count = lax.axis_size("blk")
    at = lax.axis_index("blk")
    me = lax.axis_index("comp")
    who = jnp.stack([me, at, jnp.int32(count)]).astype(I32)
    pairs = pair_tiles[0]
    forward = [(i, i + 1) for i in range(count - 1)]
    backward = [(b, a) for a, b in forward]

    messages = [sds((3 * NV + 1, CY, CZ))] * 2 + [rows_of(2)]

    idx_shape = sds((TILES, LANES), I32)
    sems = pltpu.SemaphoreType.DMA((3,))

    lo, hi, er = call(
        edge_body, "edge", messages, [HBM] * 3 + [SMEM], [HBM] * 3,
        scratch=(field(CX + 2),) + EDGE_SCRATCH + (sems,), cost_us=3.0,
    )(now, prev, kap, jh)
    state = now
    for sub in range(2):
        kept = HBM if sub == 0 else ANY
        got_lo = lax.ppermute(hi, "blk", forward)
        got_hi = lax.ppermute(lo, "blk", backward)
        inner = call(
            inner_body, "inner", [rows_of(n) for n in (2, 2, 4, 2)],
            [kept, HBM, HBM, HBM, SMEM, kept, kept], [kept] * 4,
            scratch=INNER_SCRATCH, vmem_mb=14, cost_us=4.0,
        )(state, now, prev, kap, jh, lo, hi)
        if sub == 0:
            weights, _ = lax.optimization_barrier((interp_weight[0, 0], lo))
            held = lax.all_to_all(weights, "comp", split_axis=0, concat_axis=0, tiled=True)
            didx, ridx, wide = call(
                setup_body, "setup", [idx_shape] * 2 + [sds((2, POINTS, LANES))],
                [HBM] * 3 + [SMEM, ANY], [HBM] * 3, scratch=SETUP_SCRATCH, cost_us=4.0,
            )(donor_cell[0, 0], recv_cell[0, 0], pairs, who, held)
            didx, ridx = didx.reshape(-1), ridx.reshape(-1)
        relaxed, send = call(
            finish_body, "finish", [sds(STATE), sds((16, 2, 8, LANES))],
            [kept, HBM, SMEM, SMEM, HBM, HBM, kept, kept, ANY, ANY, HBM] + [kept] * 5,
            [ANY, VMEM], scratch=FINISH_SCRATCH, vmem_mb=30, cost_us=14.0,
        )(
            state, kap, jh, who, didx, pairs, lo, hi, got_lo, got_hi, wide,
            er, *inner,
        )
        arrived = lax.all_to_all(send, "comp", split_axis=0, concat_axis=0, tiled=True)
        if sub == 0:
            state, lo, hi, er = call(
                scatter_edge_body, "scatter_edge", [sds(STATE)] + messages,
                [ANY, VMEM, HBM, HBM, HBM, HBM, SMEM], [ANY] * 4,
                scratch=SCATTER_SCRATCH + (field(CX + 2),) + EDGE_SCRATCH + (sems,),
                vmem_mb=20, cost_us=12.0,
            )(relaxed, arrived, ridx, now, prev, kap, jh)
        else:
            state = call(
                scatter_body, "scatter", sds(STATE), [ANY, VMEM, HBM], HBM,
                scratch=SCATTER_SCRATCH + (sems,), vmem_mb=12, cost_us=10.0,
            )(relaxed, arrived, ridx)
    return state[None]


def solution(mesh):
    in_specs = (
        P("comp", None, "blk", None, None),
        P("comp", None, "blk", None, None),
        P("comp", "blk", None, None),
        P("comp", None, None, None),
        P("comp", "blk", None, None, None, None),
        P("comp", "blk", None, None, None, None),
        P("comp", "blk", None, None, None),
        P("blk", None, None),
    )
    out_specs = P("comp", None, "blk", None, None)
    return jax.shard_map(shards, mesh=mesh, in_specs=in_specs, out_specs=out_specs, check_vma=False)
```

```python
import functools

import jax
import jax.numpy as jnp
from jax import lax
from jax.experimental import pallas as pl
from jax.experimental.pallas import tpu as pltpu
from jax.sharding import PartitionSpec as P

F32 = jnp.float32
I32 = jnp.int32
NV, CX, CY, CZ = 6, 8, 32, 256
LANES = 128
TILES = 32
POINTS = TILES * LANES
NT = CY // 8
YGROUPS = 11
DONOR_ROWS = 2 * YGROUPS * CZ
RECV_GROUPS = 2 * (CX - 1)
RECV_ROWS = RECV_GROUPS * CZ
PSEUDO_DIAG = 2.5
VMEM = pl.BlockSpec(memory_space=pltpu.VMEM)
SMEM = pl.BlockSpec(memory_space=pltpu.SMEM)
HBM = pl.BlockSpec(memory_space=pltpu.HBM)
ANY = pl.BlockSpec(memory_space=pl.ANY)
PADY = CY + 16
HALF = CZ // 2


def sds(shape, dtype=F32):
    return jax.ShapeDtypeStruct(shape, dtype)


def field(rows):
    return pltpu.VMEM((NV, rows, 2, PADY, LANES), F32)


def half_of(h):
    return pl.ds(LANES * h, LANES)


def call(body, name, outs, ins, out_specs, scratch=(), vmem_mb=12, cost_us=1.0):
    outs = jax.tree.map(
        lambda o, spec: pltpu.HBM(o.shape, o.dtype) if spec is HBM else o, outs, out_specs
    )
    kernel = pl.pallas_call(
        body,
        out_shape=outs,
        in_specs=ins,
        out_specs=out_specs,
        scratch_shapes=list(scratch),
        compiler_params=pltpu.CompilerParams(vmem_limit_bytes=vmem_mb << 20),
        cost_estimate=pl.CostEstimate(
            flops=0, transcendentals=0, bytes_accessed=int(cost_us * 3.0e6)
        ),
        name=name,
    )

    def run(*args):
        return kernel(*[
            pltpu.with_memory_space_constraint(a, pltpu.HBM) if spec is HBM else a
            for a, spec in zip(args, ins, strict=True)
        ])

    return run


class Copies:
    def __init__(self, sem):
        self.sem, self.list = sem, []

    def add(self, src, dst):
        c = pltpu.make_async_copy(src, dst, self.sem)
        c.start()
        self.list.append(c)

    def halves(self, src, dst):
        n = len(src.shape) - 2
        for h in range(2):
            full = (slice(None),) * n
            self.add(
                src.at[full + (slice(None), pl.ds(LANES * h, LANES))],
                dst.at[full + (h, pl.ds(8, CY), slice(None))],
            )

    def halves_out(self, src, dst):
        n = len(dst.shape) - 2
        for h in range(2):
            full = (slice(None),) * n
            self.add(
                src.at[full + (h, pl.ds(8, CY), slice(None))],
                dst.at[full + (slice(None), pl.ds(LANES * h, LANES))],
            )

    def wait(self):
        for c in self.list:
            c.wait()
        self.list = []


def clear_pads(f, first, last):
    zero = jnp.zeros((8, LANES), F32)

    @pl.loop(first, last)
    def _(x):
        for v in range(NV):
            for h in range(2):
                f[v, x, h, 0:8, :] = zero
                f[v, x, h, PADY - 8 : PADY, :] = zero


def tile_terms(f, x, t, jh, kap):
    lane = lax.broadcasted_iota(I32, (8, LANES), 1)
    y0 = pl.multiple_of(8 * t + 8, 8)
    acc = [[None, None] for _ in range(NV)]
    centres = []
    for w in range(NV):
        c = [f[w, x, h, pl.ds(y0, 8), :] for h in range(2)]
        down = [pltpu.roll(c[h], 1, 1) for h in range(2)]
        up = [pltpu.roll(c[h], LANES - 1, 1) for h in range(2)]
        zm = [jnp.where(lane == 0, 0.0, down[0]), jnp.where(lane == 0, down[0], down[1])]
        zp = [
            jnp.where(lane == LANES - 1, up[1], up[0]),
            jnp.where(lane == LANES - 1, 0.0, up[1]),
        ]
        for h in range(2):
            xm, xp = f[w, x - 1, h, pl.ds(y0, 8), :], f[w, x + 1, h, pl.ds(y0, 8), :]
            ym, yp = f[w, x, h, pl.ds(y0 - 1, 8), :], f[w, x, h, pl.ds(y0 + 1, 8), :]
            dx, dy, dz = xp - xm, yp - ym, zp[h] - zm[h]
            beside = (xp + xm) + (yp + ym) + (zp[h] + zm[h])
            for v in range(NV):
                term = jh[v * 6 + w] * dx + jh[36 + v * 6 + w] * dy + jh[72 + v * 6 + w] * dz
                if v == w:
                    term = term - kap[h] * beside
                acc[v][h] = term if acc[v][h] is None else acc[v][h] + term
        centres.append(c)
    return acc, centres


def kap_tile(kap, k, t):
    y0 = pl.multiple_of(8 * t, 8)
    both = [kap[k, pl.ds(y0, 8), half_of(h)] for h in range(2)]
    return both, [-1.0 / (PSEUDO_DIAG + 6.0 * b) for b in both]


def each_tile(count, row_of, body):
    @pl.loop(0, count * (NT // 2))
    def _(n):
        i = n // (NT // 2)
        row = row_of(i)
        for u in range(2):
            body(i, row, 2 * (n % (NT // 2)) + u)


def start_row(f, at, kap, k, now, prev, n, t, jh, emit):
    kp, ninv = kap_tile(kap, k, t)
    acc, centres = tile_terms(f, at, t, jh, kp)
    y0 = pl.multiple_of(8 * t, 8)
    for v in range(NV):
        for h in range(2):
            c = centres[v][h]
            past = prev[v, n, pl.ds(y0, 8), half_of(h)]
            if now is None:
                own = 0.5 * (past - c)
            else:
                own = 0.5 * (3.0 * c + (past - 4.0 * now[v, n, pl.ds(y0, 8), half_of(h)]))
            r = own + acc[v][h] + (6.0 * kp[h]) * c
            emit(v, h, r, r * ninv[h])


def relax_row(f, at, rs, ra, kap, k, t, jh, emit):
    kp, ninv = kap_tile(kap, k, t)
    acc, _ = tile_terms(f, at, t, jh, kp)
    y0 = pl.multiple_of(8 * t, 8)
    for v in range(NV):
        for h in range(2):
            emit(v, h, (rs[v, ra, pl.ds(y0, 8), half_of(h)] + acc[v][h]) * ninv[h])


def edge_rows(side, f, kap, now, prev, jh, ers, es1):
    def body(i, row, t):
        y0 = pl.multiple_of(8 * t, 8)
        at = i + 2 * side

        def emit(v, h, r, s):
            ers[v, at, pl.ds(y0, 8), half_of(h)] = r
            es1[v, at, pl.ds(y0, 8), half_of(h)] = s

        start_row(f, row + 1, kap, at, now, prev, at, t, jh, emit)

    each_tile(2, lambda i: i + 6 * side, body)


def edge_load(c, side, now, prev, kap, nowb, prevb, kapb):
    x, i = 6 * side, 2 * side
    if nowb is not None:
        c.add(now.at[:, pl.ds(x, 2)], nowb.at[:, pl.ds(i, 2)])
    c.add(prev.at[:, pl.ds(x, 2)], prevb.at[:, pl.ds(i, 2)])
    c.add(kap.at[pl.ds(x, 2)], kapb.at[pl.ds(i, 2)])


def edge_send(c, side, f, kap, ers, es1, msg, er):
    outer, inner = 3 * side, 1 + side
    c.halves_out(f.at[:, 1 + (CX - 1) * side], msg.at[pl.ds(0, NV)])
    c.add(ers.at[:, outer], msg.at[pl.ds(NV, NV)])
    c.add(es1.at[:, inner], msg.at[pl.ds(2 * NV, NV)])
    c.add(kap.at[outer], msg.at[3 * NV])
    c.add(ers.at[:, inner], er.at[:, side])


def edge_zero(f):
    @pl.loop(0, CY // 8)
    def _(t):
        for v in range(NV):
            for h in range(2):
                for x in (0, CX + 1):
                    f[v, x, h, pl.ds(pl.multiple_of(8 * t + 8, 8), 8), :] = jnp.zeros((8, LANES), F32)


EDGE_SCRATCH = (
    pltpu.VMEM((NV, 4, CY, CZ), F32), pltpu.VMEM((NV, 4, CY, CZ), F32), pltpu.VMEM((4, CY, CZ), F32),
    pltpu.VMEM((NV, 4, CY, CZ), F32), pltpu.VMEM((NV, 4, CY, CZ), F32),
)


def edge_body(now, prev, kap, jh, lo, hi, er, f, nowb, prevb, kapb, ers, es1, sem):
    groups = []
    for side in range(2):
        c = Copies(sem.at[side])
        c.halves(now.at[:, pl.ds(5 * side, 3)], f.at[:, pl.ds(5 * side + 1, 3)])
        edge_load(c, side, now, prev, kap, None, prevb, kapb)
        groups.append(c)
    clear_pads(f, 1, 4)
    clear_pads(f, 6, 9)
    edge_zero(f)
    for side, msg in ((0, lo), (1, hi)):
        groups[side].wait()
        edge_rows(side, f, kapb, None, prevb, jh, ers, es1)
        edge_send(groups[side], side, f, kapb, ers, es1, msg, er)
    for c in groups:
        c.wait()


def inner_body(
    q, now, prev, kap, jh, lo, hi, rs_out, s1_out, s2_out, s3_out,
    f, nowb, prevb, kapb, rs, s1, s2, s3, sem, later=True,
):
    groups = []
    for k, x, n in ((0, 1, 4), (1, 5, 2)):
        c = Copies(sem.at[k])
        c.halves(q.at[:, pl.ds(x, n)], f.at[:, pl.ds(x - 1, n)])
        rows = pl.ds(2 + 2 * k, 2)
        if later:
            c.add(now.at[:, rows], nowb.at[:, pl.ds(2 * k, 2)])
        c.add(prev.at[:, rows], prevb.at[:, pl.ds(2 * k, 2)])
        c.add(kap.at[rows], kapb.at[pl.ds(2 * k, 2)])
        groups.append(c)
    c = groups[1]
    c.halves(lo.at[pl.ds(2 * NV, NV)], s1.at[:, 0])
    c.halves(hi.at[pl.ds(2 * NV, NV)], s1.at[:, 5])
    clear_pads(f, 1, 5)
    clear_pads(s1, 1, 5)
    clear_pads(s2, 1, 3)

    def first(i, row, t):
        def emit(v, h, r, s):
            rs[v, row, pl.ds(pl.multiple_of(8 * t, 8), 8), half_of(h)] = r
            s1[v, row + 1, h, pl.ds(pl.multiple_of(8 * t + 8, 8), 8), :] = s

        start_row(f, row + 1, kapb, row, nowb if later else None, prevb, row, t, jh, emit)

    groups[0].wait()
    each_tile(2, lambda i: i, first)
    groups[1].wait()
    each_tile(2, lambda i: i + 2, first)
    for i in range(2):
        c.add(rs.at[:, 3 * i], rs_out.at[:, i])
        c.halves_out(s1.at[:, 3 * i + 1], s1_out.at[:, i])

    def second(i, row, t):
        def emit(v, h, val):
            s2[v, i, h, pl.ds(pl.multiple_of(8 * t + 8, 8), 8), :] = val

        relax_row(s1, i + 1, rs, i, kapb, i, t, jh, emit)

    each_tile(4, lambda i: i, second)
    c.halves_out(s2, s2_out)

    def third(i, row, t):
        def emit(v, h, val):
            s3[v, i, pl.ds(pl.multiple_of(8 * t, 8), 8), half_of(h)] = val

        relax_row(s2, i + 1, rs, i + 1, kapb, i + 1, t, jh, emit)

    each_tile(2, lambda i: i, third)
    c.add(s3, s3_out)
    c.wait()


INNER_SCRATCH = (
    field(6), pltpu.VMEM((NV, 4, CY, CZ), F32), pltpu.VMEM((NV, 4, CY, CZ), F32), pltpu.VMEM((4, CY, CZ), F32),
    pltpu.VMEM((NV, 4, CY, CZ), F32), field(6), field(4), pltpu.VMEM((NV, 2, CY, CZ), F32), pltpu.SemaphoreType.DMA((2,)),
)


def fix_rows(rse, s1e, far, kape, jh, lo_ok, hi_ok):
    def body(i, row, t):
        y0 = pl.multiple_of(8 * t, 8)
        sign = jnp.where(i % 2 == 0, 1.0, -1.0).astype(F32)
        scale = jnp.where(i == 0, lo_ok, jnp.where(i == 3, hi_ok, 1.0))
        kp, ninv = kap_tile(kape, row + 1, t)
        for h in range(2):
            side = [far[w, i, pl.ds(y0, 8), half_of(h)] for w in range(NV)]
            turned = [side[w] * sign for w in range(NV)]
            for v in range(NV):
                r = rse[v, row + 1, pl.ds(y0, 8), half_of(h)] - kp[h] * side[v]
                for w in range(NV):
                    r = r + jh[v * 6 + w] * turned[w]
                rse[v, row + 1, pl.ds(y0, 8), half_of(h)] = r
                s1e[v, row + 2, h, pl.ds(pl.multiple_of(y0 + 8, 8), 8), :] = r * (ninv[h] * scale)

    each_tile(4, lambda i: i - 1 + 6 * (i // 2), body)


def finish_body(
    q, kap, jh, who, idx_in, pairs_in, own_lo, own_hi, got_lo, got_hi, w_in,
    er, rs_in, s1_in, s2_in, s3_in, qn, send,
    rse, s1e, s2e, kape, far, qb, s3, q8, tab, g, wb, idx, pairs, sem,
):
    lo_ok = jnp.where(who[1] > 0, 1.0, 0.0).astype(F32)
    hi_ok = jnp.where(who[1] < who[2] - 1, 1.0, 0.0).astype(F32)
    c, d, e, k = (Copies(sem.at[n]) for n in range(4))
    for i, msg in ((0, own_lo), (1, got_lo), (2, got_hi), (3, own_hi)):
        c.add(msg.at[pl.ds(0, NV)], far.at[:, i])
    for x, msg in ((0, got_lo), (1, own_lo), (8, own_hi), (9, got_hi)):
        c.add(msg.at[pl.ds(NV, NV)], rse.at[:, x])
    c.add(kap, kape.at[pl.ds(1, CX)])
    c.add(got_lo.at[3 * NV], kape.at[0])
    c.add(got_hi.at[3 * NV], kape.at[CX + 1])
    for x, msg in ((0, got_lo), (3, own_lo), (8, own_hi), (11, got_hi)):
        k.halves(msg.at[pl.ds(2 * NV, NV)], s1e.at[:, x])
    for i, (r, s) in enumerate(((2, 4), (7, 7))):
        k.add(er.at[:, i], rse.at[:, r])
        k.add(rs_in.at[:, i], rse.at[:, (3, 6)[i]])
        k.halves(s1_in.at[:, i], s1e.at[:, s])
    d.halves(s2_in, s2e.at[:, pl.ds(3, 4)])
    d.add(q, qb)
    d.add(s3_in, s3)
    e.add(w_in, wb)
    e.add(idx_in, idx)
    e.add(pairs_in, pairs)
    clear_pads(s1e, 1, 4)
    clear_pads(s1e, 8, 11)
    clear_pads(s2e, 1, 4)
    clear_pads(s2e, 6, 9)
    c.wait()

    fix_rows(rse, s1e, far, kape, jh, lo_ok, hi_ok)
    k.wait()

    def second(i, row, t):
        scale = jnp.where(i == 0, lo_ok, jnp.where(i == 5, hi_ok, 1.0))

        def emit(v, h, val):
            s2e[v, row + 1, h, pl.ds(pl.multiple_of(8 * t + 8, 8), 8), :] = val * scale

        relax_row(s1e, row + 2, rse, row + 1, kape, row + 1, t, jh, emit)

    each_tile(6, lambda i: i - 1 + 4 * (i // 3), second)
    d.wait()

    def put(row, v, h, t, val):
        qb[v, row, pl.ds(pl.multiple_of(8 * t, 8), 8), half_of(h)] = val
        q8[row, h, pl.ds(64 * t + v, 8, stride=8), :] = val

    def third(i, row, t):
        def emit(v, h, val):
            put(row, v, h, t, qb[v, row, pl.ds(pl.multiple_of(8 * t, 8), 8), half_of(h)] + val)

        relax_row(s2e, row + 1, rse, row + 1, kape, row + 1, t, jh, emit)

    each_tile(6, lambda i: i + 2 * (i // 3), third)

    def rest(i, row, t):
        y0 = pl.multiple_of(8 * t, 8)
        for v in range(NV):
            for h in range(2):
                put(row, v, h, t, qb[v, row, pl.ds(y0, 8), half_of(h)] + s3[v, i, pl.ds(y0, 8), half_of(h)])

    each_tile(2, lambda i: i + 3, rest)
    d.add(qb, qn)
    gather_points(idx, pairs, who[0], wb, e, send, q8, tab, g)
    d.wait()


FINISH_SCRATCH = (
    pltpu.VMEM((NV, CX + 2, CY, CZ), F32), field(CX + 4), field(CX + 2), pltpu.VMEM((CX + 2, CY, CZ), F32),
    pltpu.VMEM((NV, 4, CY, CZ), F32), pltpu.VMEM((NV, CX, CY, CZ), F32), pltpu.VMEM((NV, 2, CY, CZ), F32),
    pltpu.VMEM((CX, 2, 8 * CY, LANES), F32),
    pltpu.VMEM((DONOR_ROWS + 8, LANES), F32),
    pltpu.VMEM((2 * POINTS, LANES), F32),
    pltpu.VMEM((2, POINTS, LANES), F32),
    pltpu.SMEM((POINTS,), I32),
    pltpu.SMEM((16, 16), I32),
    pltpu.SemaphoreType.DMA((4,)),
)


def gather_points(idx, pairs, me, wb, loads, send, q8, tab, g):
    @pl.loop(0, YGROUPS)
    def _(yg):
        first = pl.multiple_of(jnp.minimum(yg * 3, CY - 4) * 8, 8)
        for xg in range(2):
            for h in range(2):
                block = [q8[xg * 3 + xx, h, pl.ds(first, 32), :] for xx in range(4)]
                row = pl.multiple_of((xg * YGROUPS + yg) * CZ + h * LANES, LANES)
                tab[pl.ds(row, LANES), :] = jnp.concatenate(block, axis=0).T

    loads.wait()

    @pl.loop(0, TILES)
    def _(tile):
        @pl.when(tile % 2 < pairs[me, tile // 2])
        def _():
            @pl.loop(0, LANES // 64)
            def _(b):
                for u in range(64):
                    row = idx[pl.multiple_of(tile * LANES + b * 64, 64) + u]
                    at = pl.multiple_of(tile * 256 + b * 128, 128) + 2 * u
                    g[pl.ds(at, 2), :] = tab[pl.ds(row, 2), :]

    @pl.loop(0, TILES // 8)
    def _(n):
        for u in range(8):
            o = pl.multiple_of(n * 8 * LANES + u * LANES, LANES)
            here = g[pl.ds(o * 2, LANES, stride=2), :] * wb[0, pl.ds(o, LANES), :]
            here = here + g[pl.ds(o * 2 + 1, LANES, stride=2), :] * wb[1, pl.ds(o, LANES), :]
            turned = here.T
            parts = [turned[8 * k : 8 * k + 8] for k in range(16)]
            while len(parts) > 1:
                parts = [a + b for a, b in zip(parts[::2], parts[1::2])]
            send[4 * n + u // 2, u % 2] = parts[0]


def setup_body(
    donor_in, recv_in, pairs_in, who, held_in, didx_out, ridx_out, w_out,
    donor, recv, pairs, held, didx, dpos, ridx, w, sem,
):
    c = Copies(sem.at[0])
    c.add(donor_in, donor)
    c.add(recv_in, recv)
    c.add(pairs_in, pairs)
    d = Copies(sem.at[1])
    d.add(held_in, held)
    c.wait()
    me = who[0]
    for s in range(16):
        live = pairs[s, me]
        for t in range(2):
            i = 2 * s + t
            cell = donor[s, t, 0:1, :]
            x, y, z = cell >> 13, (cell >> 8) & (CY - 1), cell & (CZ - 1)
            xg = jnp.where(x >= 3, 1, 0)
            yg = (y * 11) >> 5
            didx[i : i + 1, :] = (xg * YGROUPS + yg) * CZ + z
            dpos[i : i + 1, :] = (x - 3 * xg) * 4 + (y - jnp.minimum(yg * 3, CY - 4))
            cell = recv[s, t : t + 1, :]
            x, y, z = cell >> 13, (cell >> 8) & (CY - 1), cell & (CZ - 1)
            row = (2 * x + (y >> 4)) * CZ + z
            row = jnp.where(t < live, row, RECV_ROWS)
            ridx[i : i + 1, :] = row * 16 + (y & 15)
    c.add(didx, didx_out)
    c.add(ridx, ridx_out)
    d.wait()

    def weigh(tile, u):
        kpos = lax.broadcasted_iota(I32, (16, LANES), 0)
        base = jnp.broadcast_to(dpos[pl.ds(tile, 1), :], (16, LANES))
        o = pl.multiple_of(tile * LANES, LANES)
        for l in range(2):
            grid = jnp.zeros((16, LANES), F32)
            for i in range(2):
                for j in range(2):
                    k = 4 * i + 2 * j + l
                    row = jnp.broadcast_to(held[tile // 2, u, k : k + 1, :], (16, LANES))
                    grid = jnp.where(kpos == base + (4 * i + j), row, grid)
            wide = [jnp.broadcast_to(grid[k : k + 1], (8, LANES)) for k in range(16)]
            w[l, pl.ds(o, LANES), :] = jnp.concatenate(wide, axis=0).T

    for part in range(4):

        @pl.loop(0, TILES // 16)
        def _(m):
            for u in range(4):
                weigh(part * (TILES // 4) + 4 * m + u, u % 2)

        rows = pl.ds(part * (POINTS // 4), POINTS // 4)
        d.add(w.at[:, rows], w_out.at[:, rows])
    c.wait()
    d.wait()


SETUP_SCRATCH = (
    pltpu.VMEM((16, 2, 8, LANES), I32),
    pltpu.VMEM((16, 2, LANES), I32),
    pltpu.SMEM((16, 16), I32),
    pltpu.VMEM((16, 2, 8, LANES), F32),
    pltpu.VMEM((TILES, LANES), I32),
    pltpu.VMEM((TILES, LANES), I32),
    pltpu.VMEM((TILES, LANES), I32),
    pltpu.VMEM((2, POINTS, LANES), F32),
    pltpu.SemaphoreType.DMA((2,)),
)


def scatter_points(vals, ridx, qb, arrive, loads, write, vrep, u, ut, half=None):
    mark = lax.broadcasted_iota(I32, (8, LANES), 0) == NV
    lane = lax.broadcasted_iota(I32, (1, LANES), 1) >> 3

    @pl.loop(0, RECV_ROWS // LANES)
    def _(i):
        u[pl.ds(pl.multiple_of(i * LANES, LANES), LANES), :] = jnp.zeros((LANES, LANES), F32)

    @pl.loop(0, TILES // 8)
    def _(n):
        for k in range(8):
            v = jnp.where(mark, 1.0, vals[4 * n + k // 2, k % 2])
            rows = pl.ds(pl.multiple_of(n * 8 * LANES + k * LANES, LANES), LANES)
            vrep[rows, :] = jnp.concatenate([v] * 16, axis=0).T

    loads.wait()

    @pl.loop(0, POINTS // 64)
    def _(b):
        for j in range(64):
            at = pl.multiple_of(b * 64, 64) + j
            word = ridx[at]
            mask = (jnp.full((1, LANES), word, I32) & 15) == lane
            pltpu.store(u.at[pl.ds(word >> 4, 1), :], vrep[pl.ds(at, 1), :], mask=mask)

    @pl.loop(0, CX - 1)
    def _(x):
        for yh in range(2):
            for h in range(2):
                row = pl.multiple_of((2 * x + yh) * CZ + h * LANES, LANES)
                ut[2 * x + yh, h] = u[pl.ds(row, LANES), :].T

    arrive.wait()

    def merge(x):
        for yh in range(2):
            for h in range(2):
                for t in range(2):
                    part = ut.at[2 * x + yh, h]
                    hit = part[pl.ds(64 * t + NV, 8, stride=8), :] != 0.0
                    y = 16 * yh + 8 * t
                    for v in range(NV):
                        new = part[pl.ds(64 * t + v, 8, stride=8), :]
                        old = qb[v, x, y : y + 8, half_of(h)]
                        write(v, x, h, y, jnp.where(hit, new, old))

    pl.loop(0, 4)(merge)
    if half is not None:
        half()
    pl.loop(4, CX - 1)(merge)


def scatter_body(q, vals, ridx_in, out, qb, vrep, u, ut, ridx, sem):
    c, e = Copies(sem.at[0]), Copies(sem.at[2])
    e.add(ridx_in, ridx)
    c.add(q, qb)

    def write(v, x, h, y, val):
        qb[v, x, y : y + 8, half_of(h)] = val

    def half():
        c.add(qb.at[:, pl.ds(0, 4)], out.at[:, pl.ds(0, 4)])

    scatter_points(vals, ridx, qb, c, e, write, vrep, u, ut, half)
    c.add(qb.at[:, pl.ds(4, 4)], out.at[:, pl.ds(4, 4)])
    c.wait()


def scatter_edge_body(
    q, vals, ridx_in, now, prev, kap, jh, out, lo, hi, er,
    qb, vrep, u, ut, ridx, f, nowb, prevb, kapb, ers, es1, sem,
):
    c, e = Copies(sem.at[0]), Copies(sem.at[2])
    e.add(ridx_in, ridx)
    c.add(q, qb)
    d = Copies(sem.at[1])
    for side in range(2):
        edge_load(d, side, now, prev, kap, nowb, prevb, kapb)
    clear_pads(f, 1, 4)
    clear_pads(f, 6, 9)
    edge_zero(f)

    def write(v, x, h, y, val):
        f[v, x + 1, h, 8 + y : 16 + y, :] = val

    scatter_points(vals, ridx, qb, c, e, write, vrep, u, ut)
    for v in range(NV):
        for h in range(2):
            f[v, CX, h, 8 : 8 + CY, :] = qb[v, CX - 1, :, half_of(h)]
    c.halves_out(f.at[:, pl.ds(1, CX)], out)
    d.wait()
    for side, msg in ((0, lo), (1, hi)):
        edge_rows(side, f, kapb, nowb, prevb, jh, ers, es1)
        edge_send(d, side, f, kapb, ers, es1, msg, er)
    d.wait()
    c.wait()


STATE = (NV, CX, CY, CZ)
SCATTER_SCRATCH = (
    pltpu.VMEM((NV, CX, CY, CZ), F32),
    pltpu.VMEM((POINTS, LANES), F32),
    pltpu.VMEM((RECV_ROWS + 8, LANES), F32),
    pltpu.VMEM((RECV_GROUPS, 2, LANES, LANES), F32),
    pltpu.SMEM((POINTS,), I32),
)


def rows_of(n):
    return sds((NV, n, CY, CZ))


def shards(
    state_now, state_prev, viscosity, jacobian, donor_cell, interp_weight, recv_cell, pair_tiles
):
    now = state_now[0]
    prev = state_prev[0]
    kap = viscosity[0]
    jh = (jacobian[0] * 0.5).reshape(-1)
    count = lax.axis_size("blk")
    at = lax.axis_index("blk")
    me = lax.axis_index("comp")
    who = jnp.stack([me, at, jnp.int32(count)]).astype(I32)
    pairs = pair_tiles[0]
    forward = [(i, i + 1) for i in range(count - 1)]
    backward = [(b, a) for a, b in forward]

    messages = [sds((3 * NV + 1, CY, CZ))] * 2 + [rows_of(2)]

    idx_shape = sds((TILES, LANES), I32)
    sems = pltpu.SemaphoreType.DMA((3,))

    held = lax.all_to_all(interp_weight[0, 0], "comp", split_axis=0, concat_axis=0, tiled=True)
    jh, held = lax.optimization_barrier((jh, held))
    lo, hi, er = call(
        edge_body, "edge", messages, [HBM] * 3 + [SMEM], [ANY] * 3,
        scratch=(field(CX + 2),) + EDGE_SCRATCH + (sems,), cost_us=3.0,
    )(now, prev, kap, jh)
    state = now
    for sub in range(2):
        got_lo = lax.ppermute(hi, "blk", forward)
        got_hi = lax.ppermute(lo, "blk", backward)
        inner = call(
            functools.partial(inner_body, later=sub > 0), "inner", [rows_of(n) for n in (2, 2, 4, 2)],
            [HBM if sub == 0 else ANY, HBM, HBM, HBM, SMEM, ANY, ANY], [ANY] * 4,
            scratch=INNER_SCRATCH, vmem_mb=14, cost_us=4.0,
        )(state, now, prev, kap, jh, lo, hi)
        if sub == 0:
            didx, ridx, wide = call(
                setup_body, "setup", [idx_shape] * 2 + [sds((2, POINTS, LANES))],
                [HBM] * 3 + [SMEM, ANY], [HBM] * 3, scratch=SETUP_SCRATCH, cost_us=4.0,
            )(donor_cell[0, 0], recv_cell[0, 0], pairs, who, held)
            didx, ridx = didx.reshape(-1), ridx.reshape(-1)
        relaxed, send = call(
            finish_body, "finish", [sds(STATE), sds((16, 2, 8, LANES))],
            [HBM if sub == 0 else ANY, HBM, SMEM, SMEM, HBM, HBM] + [ANY] * 4 + [HBM] + [ANY] * 5,
            [ANY, VMEM], scratch=FINISH_SCRATCH, vmem_mb=30, cost_us=14.0,
        )(
            state, kap, jh, who, didx, pairs, lo, hi, got_lo, got_hi, wide,
            er, *inner,
        )
        arrived = lax.all_to_all(send, "comp", split_axis=0, concat_axis=0, tiled=True)
        if sub == 0:
            state, lo, hi, er = call(
                scatter_edge_body, "scatter_edge", [sds(STATE)] + messages,
                [ANY, VMEM, HBM, HBM, HBM, HBM, SMEM], [ANY] * 4,
                scratch=SCATTER_SCRATCH + (field(CX + 2),) + EDGE_SCRATCH + (sems,),
                vmem_mb=20, cost_us=12.0,
            )(relaxed, arrived, ridx, now, prev, kap, jh)
        else:
            state = call(
                scatter_body, "scatter", sds(STATE), [ANY, VMEM, HBM], HBM,
                scratch=SCATTER_SCRATCH + (sems,), vmem_mb=12, cost_us=10.0,
            )(relaxed, arrived, ridx)
    return state[None]


def solution(mesh):
    in_specs = (
        P("comp", None, "blk", None, None),
        P("comp", None, "blk", None, None),
        P("comp", "blk", None, None),
        P("comp", None, None, None),
        P("comp", "blk", None, None, None, None),
        P("comp", "blk", None, None, None, None),
        P("comp", "blk", None, None, None),
        P("blk", None, None),
    )
    out_specs = P("comp", None, "blk", None, None)
    return jax.shard_map(shards, mesh=mesh, in_specs=in_specs, out_specs=out_specs, check_vma=False)
```

```python
import functools

import jax
import jax.numpy as jnp
from jax import lax
from jax.experimental import pallas as pl
from jax.experimental.pallas import tpu as pltpu
from jax.sharding import PartitionSpec as P

F32 = jnp.float32
I32 = jnp.int32
NV, CX, CY, CZ = 6, 8, 32, 256
LANES = 128
TILES = 32
POINTS = TILES * LANES
NT = CY // 8
YGROUPS = 11
DONOR_ROWS = 2 * YGROUPS * CZ
RECV_GROUPS = 2 * (CX - 1)
RECV_ROWS = RECV_GROUPS * CZ
PSEUDO_DIAG = 2.5
VMEM = pl.BlockSpec(memory_space=pltpu.VMEM)
SMEM = pl.BlockSpec(memory_space=pltpu.SMEM)
HBM = pl.BlockSpec(memory_space=pltpu.HBM)
ANY = pl.BlockSpec(memory_space=pl.ANY)
PADY = CY + 16
HALF = CZ // 2


def sds(shape, dtype=F32):
    return jax.ShapeDtypeStruct(shape, dtype)


def field(rows):
    return pltpu.VMEM((NV, rows, 2, PADY, LANES), F32)


def half_of(h):
    return pl.ds(LANES * h, LANES)


def call(body, name, outs, ins, out_specs, scratch=(), vmem_mb=12, cost_us=1.0):
    outs = jax.tree.map(
        lambda o, spec: pltpu.HBM(o.shape, o.dtype) if spec is HBM else o, outs, out_specs
    )
    kernel = pl.pallas_call(
        body,
        out_shape=outs,
        in_specs=ins,
        out_specs=out_specs,
        scratch_shapes=list(scratch),
        compiler_params=pltpu.CompilerParams(vmem_limit_bytes=vmem_mb << 20),
        cost_estimate=pl.CostEstimate(
            flops=0, transcendentals=0, bytes_accessed=int(cost_us * 3.0e6)
        ),
        name=name,
    )

    def run(*args):
        return kernel(*[
            pltpu.with_memory_space_constraint(a, pltpu.HBM) if spec is HBM else a
            for a, spec in zip(args, ins, strict=True)
        ])

    return run


class Copies:
    def __init__(self, sem):
        self.sem, self.list = sem, []

    def add(self, src, dst):
        c = pltpu.make_async_copy(src, dst, self.sem)
        c.start()
        self.list.append(c)

    def halves(self, src, dst):
        n = len(src.shape) - 2
        for h in range(2):
            full = (slice(None),) * n
            self.add(
                src.at[full + (slice(None), pl.ds(LANES * h, LANES))],
                dst.at[full + (h, pl.ds(8, CY), slice(None))],
            )

    def halves_out(self, src, dst):
        n = len(dst.shape) - 2
        for h in range(2):
            full = (slice(None),) * n
            self.add(
                src.at[full + (h, pl.ds(8, CY), slice(None))],
                dst.at[full + (slice(None), pl.ds(LANES * h, LANES))],
            )

    def wait(self):
        for c in self.list:
            c.wait()
        self.list = []


def clear_pads(f, first, last):
    zero = jnp.zeros((8, LANES), F32)

    @pl.loop(first, last)
    def _(x):
        for v in range(NV):
            for h in range(2):
                f[v, x, h, 0:8, :] = zero
                f[v, x, h, PADY - 8 : PADY, :] = zero


def tile_terms(f, x, t, jh, kap):
    lane = lax.broadcasted_iota(I32, (8, LANES), 1)
    y0 = pl.multiple_of(8 * t + 8, 8)
    acc = [[None, None] for _ in range(NV)]
    centres = []
    for w in range(NV):
        c = [f[w, x, h, pl.ds(y0, 8), :] for h in range(2)]
        down = [pltpu.roll(c[h], 1, 1) for h in range(2)]
        up = [pltpu.roll(c[h], LANES - 1, 1) for h in range(2)]
        zm = [jnp.where(lane == 0, 0.0, down[0]), jnp.where(lane == 0, down[0], down[1])]
        zp = [
            jnp.where(lane == LANES - 1, up[1], up[0]),
            jnp.where(lane == LANES - 1, 0.0, up[1]),
        ]
        for h in range(2):
            xm, xp = f[w, x - 1, h, pl.ds(y0, 8), :], f[w, x + 1, h, pl.ds(y0, 8), :]
            ym, yp = f[w, x, h, pl.ds(y0 - 1, 8), :], f[w, x, h, pl.ds(y0 + 1, 8), :]
            dx, dy, dz = xp - xm, yp - ym, zp[h] - zm[h]
            beside = (xp + xm) + (yp + ym) + (zp[h] + zm[h])
            for v in range(NV):
                term = jh[v * 6 + w] * dx + jh[36 + v * 6 + w] * dy + jh[72 + v * 6 + w] * dz
                if v == w:
                    term = term - kap[h] * beside
                acc[v][h] = term if acc[v][h] is None else acc[v][h] + term
        centres.append(c)
    return acc, centres


def kap_tile(kap, k, t):
    y0 = pl.multiple_of(8 * t, 8)
    both = [kap[k, pl.ds(y0, 8), half_of(h)] for h in range(2)]
    return both, [-1.0 / (PSEUDO_DIAG + 6.0 * b) for b in both]


def each_tile(count, row_of, body):
    @pl.loop(0, count * (NT // 2))
    def _(n):
        i = n // (NT // 2)
        row = row_of(i)
        for u in range(2):
            body(i, row, 2 * (n % (NT // 2)) + u)


def start_row(f, at, kap, k, now, prev, n, t, jh, emit):
    kp, ninv = kap_tile(kap, k, t)
    acc, centres = tile_terms(f, at, t, jh, kp)
    y0 = pl.multiple_of(8 * t, 8)
    for v in range(NV):
        for h in range(2):
            c = centres[v][h]
            past = prev[v, n, pl.ds(y0, 8), half_of(h)]
            if now is None:
                own = 0.5 * (past - c)
            else:
                own = 0.5 * (3.0 * c + (past - 4.0 * now[v, n, pl.ds(y0, 8), half_of(h)]))
            r = own + acc[v][h] + (6.0 * kp[h]) * c
            emit(v, h, r, r * ninv[h])


def relax_row(f, at, rs, ra, kap, k, t, jh, emit):
    kp, ninv = kap_tile(kap, k, t)
    acc, _ = tile_terms(f, at, t, jh, kp)
    y0 = pl.multiple_of(8 * t, 8)
    for v in range(NV):
        for h in range(2):
            emit(v, h, (rs[v, ra, pl.ds(y0, 8), half_of(h)] + acc[v][h]) * ninv[h])


def edge_rows(side, f, kap, now, prev, jh, ers, es1):
    def body(i, row, t):
        y0 = pl.multiple_of(8 * t, 8)
        at = i + 2 * side

        def emit(v, h, r, s):
            ers[v, at, pl.ds(y0, 8), half_of(h)] = r
            es1[v, at, pl.ds(y0, 8), half_of(h)] = s

        start_row(f, row + 1, kap, at, now, prev, at, t, jh, emit)

    each_tile(2, lambda i: i + 6 * side, body)


def edge_load(c, side, now, prev, kap, nowb, prevb, kapb):
    x, i = 6 * side, 2 * side
    if nowb is not None:
        c.add(now.at[:, pl.ds(x, 2)], nowb.at[:, pl.ds(i, 2)])
    c.add(prev.at[:, pl.ds(x, 2)], prevb.at[:, pl.ds(i, 2)])
    c.add(kap.at[pl.ds(x, 2)], kapb.at[pl.ds(i, 2)])


def edge_send(c, side, f, kap, ers, es1, msg, er):
    outer, inner = 3 * side, 1 + side
    c.halves_out(f.at[:, 1 + (CX - 1) * side], msg.at[pl.ds(0, NV)])
    c.add(ers.at[:, outer], msg.at[pl.ds(NV, NV)])
    c.add(es1.at[:, inner], msg.at[pl.ds(2 * NV, NV)])
    if msg.shape[0] > 3 * NV:
        c.add(kap.at[outer], msg.at[3 * NV])
    c.add(ers.at[:, inner], er.at[:, side])


def edge_zero(f):
    @pl.loop(0, CY // 8)
    def _(t):
        for v in range(NV):
            for h in range(2):
                for x in (0, CX + 1):
                    f[v, x, h, pl.ds(pl.multiple_of(8 * t + 8, 8), 8), :] = jnp.zeros((8, LANES), F32)


EDGE_SCRATCH = (
    pltpu.VMEM((NV, 4, CY, CZ), F32), pltpu.VMEM((NV, 4, CY, CZ), F32), pltpu.VMEM((4, CY, CZ), F32),
    pltpu.VMEM((NV, 4, CY, CZ), F32), pltpu.VMEM((NV, 4, CY, CZ), F32),
)


def edge_body(now, prev, kap, jh, lo, hi, er, f, nowb, prevb, kapb, ers, es1, sem):
    groups = []
    for side in range(2):
        c = Copies(sem.at[side])
        c.halves(now.at[:, pl.ds(5 * side, 3)], f.at[:, pl.ds(5 * side + 1, 3)])
        edge_load(c, side, now, prev, kap, None, prevb, kapb)
        groups.append(c)
    clear_pads(f, 1, 4)
    clear_pads(f, 6, 9)
    edge_zero(f)
    for side, msg in ((0, lo), (1, hi)):
        groups[side].wait()
        edge_rows(side, f, kapb, None, prevb, jh, ers, es1)
        edge_send(groups[side], side, f, kapb, ers, es1, msg, er)
    for c in groups:
        c.wait()


def inner_body(
    q, now, prev, kap, jh, lo, hi, rs_out, s1_out, s2_out, s3_out,
    f, nowb, prevb, kapb, rs, s1, s2, s3, sem, later=True,
):
    groups = []
    for k, x, n in ((0, 1, 4), (1, 5, 2)):
        c = Copies(sem.at[k])
        c.halves(q.at[:, pl.ds(x, n)], f.at[:, pl.ds(x - 1, n)])
        rows = pl.ds(2 + 2 * k, 2)
        if later:
            c.add(now.at[:, rows], nowb.at[:, pl.ds(2 * k, 2)])
        c.add(prev.at[:, rows], prevb.at[:, pl.ds(2 * k, 2)])
        c.add(kap.at[rows], kapb.at[pl.ds(2 * k, 2)])
        groups.append(c)
    c = groups[1]
    c.halves(lo.at[pl.ds(2 * NV, NV)], s1.at[:, 0])
    c.halves(hi.at[pl.ds(2 * NV, NV)], s1.at[:, 5])
    clear_pads(f, 1, 5)
    clear_pads(s1, 1, 5)
    clear_pads(s2, 1, 3)

    def first(i, row, t):
        def emit(v, h, r, s):
            rs[v, row, pl.ds(pl.multiple_of(8 * t, 8), 8), half_of(h)] = r
            s1[v, row + 1, h, pl.ds(pl.multiple_of(8 * t + 8, 8), 8), :] = s

        start_row(f, row + 1, kapb, row, nowb if later else None, prevb, row, t, jh, emit)

    groups[0].wait()
    each_tile(2, lambda i: i, first)
    groups[1].wait()
    each_tile(2, lambda i: i + 2, first)
    for i in range(2):
        c.add(rs.at[:, 3 * i], rs_out.at[:, i])
        c.halves_out(s1.at[:, 3 * i + 1], s1_out.at[:, i])

    def second(i, row, t):
        def emit(v, h, val):
            s2[v, i, h, pl.ds(pl.multiple_of(8 * t + 8, 8), 8), :] = val

        relax_row(s1, i + 1, rs, i, kapb, i, t, jh, emit)

    each_tile(4, lambda i: i, second)
    c.halves_out(s2, s2_out)

    def third(i, row, t):
        def emit(v, h, val):
            s3[v, i, pl.ds(pl.multiple_of(8 * t, 8), 8), half_of(h)] = val

        relax_row(s2, i + 1, rs, i + 1, kapb, i + 1, t, jh, emit)

    each_tile(2, lambda i: i, third)
    c.add(s3, s3_out)
    c.wait()


INNER_SCRATCH = (
    field(6), pltpu.VMEM((NV, 4, CY, CZ), F32), pltpu.VMEM((NV, 4, CY, CZ), F32), pltpu.VMEM((4, CY, CZ), F32),
    pltpu.VMEM((NV, 4, CY, CZ), F32), field(6), field(4), pltpu.VMEM((NV, 2, CY, CZ), F32), pltpu.SemaphoreType.DMA((2,)),
)


def fix_rows(rse, s1e, far, kape, jh, lo_ok, hi_ok):
    def body(i, row, t):
        y0 = pl.multiple_of(8 * t, 8)
        sign = jnp.where(i % 2 == 0, 1.0, -1.0).astype(F32)
        scale = jnp.where(i == 0, lo_ok, jnp.where(i == 3, hi_ok, 1.0))
        kp, ninv = kap_tile(kape, row + 1, t)
        for h in range(2):
            side = [far[w, i, pl.ds(y0, 8), half_of(h)] for w in range(NV)]
            turned = [side[w] * sign for w in range(NV)]
            for v in range(NV):
                r = rse[v, row + 1, pl.ds(y0, 8), half_of(h)] - kp[h] * side[v]
                for w in range(NV):
                    r = r + jh[v * 6 + w] * turned[w]
                rse[v, row + 1, pl.ds(y0, 8), half_of(h)] = r
                s1e[v, row + 2, h, pl.ds(pl.multiple_of(y0 + 8, 8), 8), :] = r * (ninv[h] * scale)

    each_tile(4, lambda i: i - 1 + 6 * (i // 2), body)


def finish_body(
    q, kap, jh, who, idx_in, pairs_in, own_lo, own_hi, got_lo, got_hi, klo, khi, w_in,
    er, rs_in, s1_in, s2_in, s3_in, qn, send,
    rse, s1e, s2e, kape, far, qb, s3, q8, tab, g, wb, idx, pairs, sem,
):
    lo_ok = jnp.where(who[1] > 0, 1.0, 0.0).astype(F32)
    hi_ok = jnp.where(who[1] < who[2] - 1, 1.0, 0.0).astype(F32)
    c, d, e, k = (Copies(sem.at[n]) for n in range(4))
    for i, msg in ((0, own_lo), (1, got_lo), (2, got_hi), (3, own_hi)):
        c.add(msg.at[pl.ds(0, NV)], far.at[:, i])
    for x, msg in ((0, got_lo), (1, own_lo), (8, own_hi), (9, got_hi)):
        c.add(msg.at[pl.ds(NV, NV)], rse.at[:, x])
    c.add(kap, kape.at[pl.ds(1, CX)])
    c.add(klo.at[3 * NV], kape.at[0])
    c.add(khi.at[3 * NV], kape.at[CX + 1])
    for x, msg in ((0, got_lo), (3, own_lo), (8, own_hi), (11, got_hi)):
        k.halves(msg.at[pl.ds(2 * NV, NV)], s1e.at[:, x])
    for i, (r, s) in enumerate(((2, 4), (7, 7))):
        k.add(er.at[:, i], rse.at[:, r])
        k.add(rs_in.at[:, i], rse.at[:, (3, 6)[i]])
        k.halves(s1_in.at[:, i], s1e.at[:, s])
    d.halves(s2_in, s2e.at[:, pl.ds(3, 4)])
    d.add(q, qb)
    d.add(s3_in, s3)
    e.add(w_in, wb)
    e.add(idx_in, idx)
    e.add(pairs_in, pairs)
    clear_pads(s1e, 1, 4)
    clear_pads(s1e, 8, 11)
    clear_pads(s2e, 1, 4)
    clear_pads(s2e, 6, 9)
    c.wait()

    fix_rows(rse, s1e, far, kape, jh, lo_ok, hi_ok)
    k.wait()

    def second(i, row, t):
        scale = jnp.where(i == 0, lo_ok, jnp.where(i == 5, hi_ok, 1.0))

        def emit(v, h, val):
            s2e[v, row + 1, h, pl.ds(pl.multiple_of(8 * t + 8, 8), 8), :] = val * scale

        relax_row(s1e, row + 2, rse, row + 1, kape, row + 1, t, jh, emit)

    each_tile(6, lambda i: i - 1 + 4 * (i // 3), second)
    d.wait()

    def put(row, v, h, t, val):
        qb[v, row, pl.ds(pl.multiple_of(8 * t, 8), 8), half_of(h)] = val
        q8[row, h, pl.ds(64 * t + v, 8, stride=8), :] = val

    def third(i, row, t):
        def emit(v, h, val):
            put(row, v, h, t, qb[v, row, pl.ds(pl.multiple_of(8 * t, 8), 8), half_of(h)] + val)

        relax_row(s2e, row + 1, rse, row + 1, kape, row + 1, t, jh, emit)

    each_tile(6, lambda i: i + 2 * (i // 3), third)

    def rest(i, row, t):
        y0 = pl.multiple_of(8 * t, 8)
        for v in range(NV):
            for h in range(2):
                put(row, v, h, t, qb[v, row, pl.ds(y0, 8), half_of(h)] + s3[v, i, pl.ds(y0, 8), half_of(h)])

    each_tile(2, lambda i: i + 3, rest)
    d.add(qb, qn)
    gather_points(idx, pairs, who[0], wb, e, send, q8, tab, g)
    d.wait()


FINISH_SCRATCH = (
    pltpu.VMEM((NV, CX + 2, CY, CZ), F32), field(CX + 4), field(CX + 2), pltpu.VMEM((CX + 2, CY, CZ), F32),
    pltpu.VMEM((NV, 4, CY, CZ), F32), pltpu.VMEM((NV, CX, CY, CZ), F32), pltpu.VMEM((NV, 2, CY, CZ), F32),
    pltpu.VMEM((CX, 2, 8 * CY, LANES), F32),
    pltpu.VMEM((DONOR_ROWS + 8, LANES), F32),
    pltpu.VMEM((2 * POINTS, LANES), F32),
    pltpu.VMEM((2, POINTS, LANES), F32),
    pltpu.SMEM((POINTS,), I32),
    pltpu.SMEM((16, 16), I32),
    pltpu.SemaphoreType.DMA((4,)),
)


def gather_points(idx, pairs, me, wb, loads, send, q8, tab, g):
    @pl.loop(0, YGROUPS)
    def _(yg):
        first = pl.multiple_of(jnp.minimum(yg * 3, CY - 4) * 8, 8)
        for xg in range(2):
            for h in range(2):
                block = [q8[xg * 3 + xx, h, pl.ds(first, 32), :] for xx in range(4)]
                row = pl.multiple_of((xg * YGROUPS + yg) * CZ + h * LANES, LANES)
                tab[pl.ds(row, LANES), :] = jnp.concatenate(block, axis=0).T

    loads.wait()

    @pl.loop(0, TILES)
    def _(tile):
        @pl.when(tile % 2 < pairs[me, tile // 2])
        def _():
            for u in range(LANES):
                row = idx[pl.multiple_of(tile * LANES, LANES) + u]
                at = pl.multiple_of(tile * 2 * LANES, 2 * LANES) + 2 * u
                g[pl.ds(at, 2), :] = tab[pl.ds(row, 2), :]

    @pl.loop(0, TILES // 8)
    def _(n):
        for u in range(8):
            o = pl.multiple_of(n * 8 * LANES + u * LANES, LANES)
            here = g[pl.ds(o * 2, LANES, stride=2), :] * wb[0, pl.ds(o, LANES), :]
            here = here + g[pl.ds(o * 2 + 1, LANES, stride=2), :] * wb[1, pl.ds(o, LANES), :]
            turned = here.T
            parts = [turned[8 * k : 8 * k + 8] for k in range(16)]
            while len(parts) > 1:
                parts = [a + b for a, b in zip(parts[::2], parts[1::2])]
            send[4 * n + u // 2, u % 2] = parts[0]


def setup_body(
    donor_in, recv_in, pairs_in, who, held_in, didx_out, ridx_out, w_out,
    donor, recv, pairs, held, didx, dpos, ridx, w, sem,
):
    c = Copies(sem.at[0])
    c.add(donor_in, donor)
    c.add(recv_in, recv)
    c.add(pairs_in, pairs)
    d = Copies(sem.at[1])
    d.add(held_in, held)
    c.wait()
    me = who[0]
    for s in range(16):
        live = pairs[s, me]
        for t in range(2):
            i = 2 * s + t
            cell = donor[s, t, 0:1, :]
            x, y, z = cell >> 13, (cell >> 8) & (CY - 1), cell & (CZ - 1)
            xg = jnp.where(x >= 3, 1, 0)
            yg = (y * 11) >> 5
            didx[i : i + 1, :] = (xg * YGROUPS + yg) * CZ + z
            dpos[i : i + 1, :] = (x - 3 * xg) * 4 + (y - jnp.minimum(yg * 3, CY - 4))
            cell = recv[s, t : t + 1, :]
            x, y, z = cell >> 13, (cell >> 8) & (CY - 1), cell & (CZ - 1)
            row = (2 * x + (y >> 4)) * CZ + z
            row = jnp.where(t < live, row, RECV_ROWS)
            ridx[i : i + 1, :] = row * 16 + (y & 15)
    c.add(didx, didx_out)
    c.add(ridx, ridx_out)
    d.wait()

    def weigh(tile, u):
        kpos = lax.broadcasted_iota(I32, (16, LANES), 0)
        base = jnp.broadcast_to(dpos[pl.ds(tile, 1), :], (16, LANES))
        o = pl.multiple_of(tile * LANES, LANES)
        for l in range(2):
            grid = jnp.zeros((16, LANES), F32)
            for i in range(2):
                for j in range(2):
                    k = 4 * i + 2 * j + l
                    row = jnp.broadcast_to(held[tile // 2, u, k : k + 1, :], (16, LANES))
                    grid = jnp.where(kpos == base + (4 * i + j), row, grid)
            wide = [jnp.broadcast_to(grid[k : k + 1], (8, LANES)) for k in range(16)]
            w[l, pl.ds(o, LANES), :] = jnp.concatenate(wide, axis=0).T

    for part in range(4):

        @pl.loop(0, TILES // 16)
        def _(m):
            for u in range(4):
                weigh(part * (TILES // 4) + 4 * m + u, u % 2)

        rows = pl.ds(part * (POINTS // 4), POINTS // 4)
        d.add(w.at[:, rows], w_out.at[:, rows])
    c.wait()
    d.wait()


SETUP_SCRATCH = (
    pltpu.VMEM((16, 2, 8, LANES), I32),
    pltpu.VMEM((16, 2, LANES), I32),
    pltpu.SMEM((16, 16), I32),
    pltpu.VMEM((16, 2, 8, LANES), F32),
    pltpu.VMEM((TILES, LANES), I32),
    pltpu.VMEM((TILES, LANES), I32),
    pltpu.VMEM((TILES, LANES), I32),
    pltpu.VMEM((2, POINTS, LANES), F32),
    pltpu.SemaphoreType.DMA((2,)),
)


def scatter_points(vals, ridx, qb, arrive, loads, write, vrep, u, ut, half=None):
    mark = lax.broadcasted_iota(I32, (8, LANES), 0) == NV
    lane = lax.broadcasted_iota(I32, (1, LANES), 1) >> 3

    @pl.loop(0, RECV_ROWS // LANES)
    def _(i):
        u[pl.ds(pl.multiple_of(i * LANES, LANES), LANES), :] = jnp.zeros((LANES, LANES), F32)

    @pl.loop(0, TILES // 8)
    def _(n):
        for k in range(8):
            v = jnp.where(mark, 1.0, vals[4 * n + k // 2, k % 2])
            rows = pl.ds(pl.multiple_of(n * 8 * LANES + k * LANES, LANES), LANES)
            vrep[rows, :] = jnp.concatenate([v] * 16, axis=0).T

    loads.wait()

    @pl.loop(0, POINTS // 64)
    def _(b):
        for j in range(64):
            at = pl.multiple_of(b * 64, 64) + j
            word = ridx[at]
            mask = (jnp.full((1, LANES), word, I32) & 15) == lane
            pltpu.store(u.at[pl.ds(word >> 4, 1), :], vrep[pl.ds(at, 1), :], mask=mask)

    @pl.loop(0, CX - 1)
    def _(x):
        for yh in range(2):
            for h in range(2):
                row = pl.multiple_of((2 * x + yh) * CZ + h * LANES, LANES)
                ut[2 * x + yh, h] = u[pl.ds(row, LANES), :].T

    arrive.wait()

    def merge(x):
        for yh in range(2):
            for h in range(2):
                for t in range(2):
                    part = ut.at[2 * x + yh, h]
                    hit = part[pl.ds(64 * t + NV, 8, stride=8), :] != 0.0
                    y = 16 * yh + 8 * t
                    for v in range(NV):
                        new = part[pl.ds(64 * t + v, 8, stride=8), :]
                        old = qb[v, x, y : y + 8, half_of(h)]
                        write(v, x, h, y, jnp.where(hit, new, old))

    pl.loop(0, 4)(merge)
    if half is not None:
        half()
    pl.loop(4, CX - 1)(merge)


def scatter_body(q, vals, ridx_in, out, qb, vrep, u, ut, ridx, sem):
    c, e = Copies(sem.at[0]), Copies(sem.at[2])
    e.add(ridx_in, ridx)
    c.add(q, qb)

    def write(v, x, h, y, val):
        qb[v, x, y : y + 8, half_of(h)] = val

    def half():
        c.add(qb.at[:, pl.ds(0, 4)], out.at[:, pl.ds(0, 4)])

    scatter_points(vals, ridx, qb, c, e, write, vrep, u, ut, half)
    c.add(qb.at[:, pl.ds(4, 4)], out.at[:, pl.ds(4, 4)])
    c.wait()


def scatter_edge_body(
    q, vals, ridx_in, now, prev, kap, jh, out, lo, hi, er,
    qb, vrep, u, ut, ridx, f, nowb, prevb, kapb, ers, es1, sem,
):
    c, e = Copies(sem.at[0]), Copies(sem.at[2])
    e.add(ridx_in, ridx)
    c.add(q, qb)
    d = Copies(sem.at[1])
    for side in range(2):
        edge_load(d, side, now, prev, kap, nowb, prevb, kapb)
    clear_pads(f, 1, 4)
    clear_pads(f, 6, 9)
    edge_zero(f)

    def write(v, x, h, y, val):
        f[v, x + 1, h, 8 + y : 16 + y, :] = val

    scatter_points(vals, ridx, qb, c, e, write, vrep, u, ut)
    for v in range(NV):
        for h in range(2):
            f[v, CX, h, 8 : 8 + CY, :] = qb[v, CX - 1, :, half_of(h)]
    c.halves_out(f.at[:, pl.ds(1, CX)], out)
    d.wait()
    for side, msg in ((0, lo), (1, hi)):
        edge_rows(side, f, kapb, nowb, prevb, jh, ers, es1)
        edge_send(d, side, f, kapb, ers, es1, msg, er)
    d.wait()
    c.wait()


STATE = (NV, CX, CY, CZ)
SCATTER_SCRATCH = (
    pltpu.VMEM((NV, CX, CY, CZ), F32),
    pltpu.VMEM((POINTS, LANES), F32),
    pltpu.VMEM((RECV_ROWS + 8, LANES), F32),
    pltpu.VMEM((RECV_GROUPS, 2, LANES, LANES), F32),
    pltpu.SMEM((POINTS,), I32),
)


def rows_of(n):
    return sds((NV, n, CY, CZ))


def shards(
    state_now, state_prev, viscosity, jacobian, donor_cell, interp_weight, recv_cell, pair_tiles
):
    now = state_now[0]
    prev = state_prev[0]
    kap = viscosity[0]
    jh = (jacobian[0] * 0.5).reshape(-1)
    count = lax.axis_size("blk")
    at = lax.axis_index("blk")
    me = lax.axis_index("comp")
    who = jnp.stack([me, at, jnp.int32(count)]).astype(I32)
    pairs = pair_tiles[0]
    forward = [(i, i + 1) for i in range(count - 1)]
    backward = [(b, a) for a, b in forward]

    def messages(planes):
        return [sds((planes, CY, CZ))] * 2 + [rows_of(2)]


    idx_shape = sds((TILES, LANES), I32)
    sems = pltpu.SemaphoreType.DMA((3,))

    lo, hi, er = call(
        edge_body, "edge", messages(3 * NV + 1), [HBM] * 3 + [SMEM], [ANY] * 3,
        scratch=(field(CX + 2),) + EDGE_SCRATCH + (sems,), cost_us=3.0,
    )(now, prev, kap, jh)
    state = now
    for sub in range(2):
        got_lo = lax.ppermute(hi, "blk", forward)
        got_hi = lax.ppermute(lo, "blk", backward)
        if sub == 0:
            klo, khi = got_lo, got_hi
            weights, lo, who = lax.optimization_barrier((interp_weight[0, 0], lo, who))
            held = lax.all_to_all(weights, "comp", split_axis=0, concat_axis=0, tiled=True)
            jh, held = lax.optimization_barrier((jh, held))
        inner = call(
            functools.partial(inner_body, later=sub > 0), "inner", [rows_of(n) for n in (2, 2, 4, 2)],
            [HBM if sub == 0 else ANY, HBM, HBM, HBM, SMEM, ANY, ANY], [ANY] * 4,
            scratch=INNER_SCRATCH, vmem_mb=14, cost_us=4.0,
        )(state, now, prev, kap, jh, lo, hi)
        if sub == 0:
            didx, ridx, wide = call(
                setup_body, "setup", [idx_shape] * 2 + [sds((2, POINTS, LANES))],
                [HBM] * 3 + [SMEM, ANY], [HBM] * 3, scratch=SETUP_SCRATCH, cost_us=4.0,
            )(donor_cell[0, 0], recv_cell[0, 0], pairs, who, held)
            didx, ridx = didx.reshape(-1), ridx.reshape(-1)
        relaxed, send = call(
            finish_body, "finish", [sds(STATE), sds((16, 2, 8, LANES))],
            [HBM if sub == 0 else ANY, HBM, SMEM, SMEM, HBM, HBM] + [ANY] * 6 + [HBM] + [ANY] * 5,
            [ANY, VMEM], scratch=FINISH_SCRATCH, vmem_mb=30, cost_us=14.0,
        )(
            state, kap, jh, who, didx, pairs, lo, hi, got_lo, got_hi, klo, khi, wide,
            er, *inner,
        )
        arrived = lax.all_to_all(send, "comp", split_axis=0, concat_axis=0, tiled=True)
        if sub == 0:
            state, lo, hi, er = call(
                scatter_edge_body, "scatter_edge", [sds(STATE)] + messages(3 * NV),
                [ANY, VMEM, HBM, HBM, HBM, HBM, SMEM], [ANY] * 4,
                scratch=SCATTER_SCRATCH + (field(CX + 2),) + EDGE_SCRATCH + (sems,),
                vmem_mb=20, cost_us=12.0,
            )(relaxed, arrived, ridx, now, prev, kap, jh)
        else:
            state = call(
                scatter_body, "scatter", sds(STATE), [ANY, VMEM, HBM], HBM,
                scratch=SCATTER_SCRATCH + (sems,), vmem_mb=12, cost_us=10.0,
            )(relaxed, arrived, ridx)
    return state[None]


def solution(mesh):
    in_specs = (
        P("comp", None, "blk", None, None),
        P("comp", None, "blk", None, None),
        P("comp", "blk", None, None),
        P("comp", None, None, None),
        P("comp", "blk", None, None, None, None),
        P("comp", "blk", None, None, None, None),
        P("comp", "blk", None, None, None),
        P("blk", None, None),
    )
    out_specs = P("comp", None, "blk", None, None)
    return jax.shard_map(shards, mesh=mesh, in_specs=in_specs, out_specs=out_specs, check_vma=False)
```

```python
import functools

import jax
import jax.numpy as jnp
from jax import lax
from jax.experimental import pallas as pl
from jax.experimental.pallas import tpu as pltpu
from jax.sharding import PartitionSpec as P

F32 = jnp.float32
I32 = jnp.int32
NV, CX, CY, CZ = 6, 8, 32, 256
LANES = 128
TILES = 32
POINTS = TILES * LANES
NT = CY // 8
YGROUPS = 11
DONOR_ROWS = 2 * YGROUPS * CZ
RECV_GROUPS = 2 * (CX - 1)
RECV_ROWS = RECV_GROUPS * CZ
PSEUDO_DIAG = 2.5
VMEM = pl.BlockSpec(memory_space=pltpu.VMEM)
SMEM = pl.BlockSpec(memory_space=pltpu.SMEM)
HBM = pl.BlockSpec(memory_space=pltpu.HBM)
ANY = pl.BlockSpec(memory_space=pl.ANY)
PADY = CY + 16
HALF = CZ // 2


def sds(shape, dtype=F32):
    return jax.ShapeDtypeStruct(shape, dtype)


def field(rows):
    return pltpu.VMEM((NV, rows, 2, PADY, LANES), F32)


def half_of(h):
    return pl.ds(LANES * h, LANES)


def call(body, name, outs, ins, out_specs, scratch=(), vmem_mb=12, cost_us=1.0):
    outs = jax.tree.map(
        lambda o, spec: pltpu.HBM(o.shape, o.dtype) if spec is HBM else o, outs, out_specs
    )
    kernel = pl.pallas_call(
        body,
        out_shape=outs,
        in_specs=ins,
        out_specs=out_specs,
        scratch_shapes=list(scratch),
        compiler_params=pltpu.CompilerParams(vmem_limit_bytes=vmem_mb << 20),
        cost_estimate=pl.CostEstimate(
            flops=0, transcendentals=0, bytes_accessed=int(cost_us * 3.0e6)
        ),
        name=name,
    )

    def run(*args):
        return kernel(*[
            pltpu.with_memory_space_constraint(a, pltpu.HBM) if spec is HBM else a
            for a, spec in zip(args, ins, strict=True)
        ])

    return run


class Copies:
    def __init__(self, sem):
        self.sem, self.list = sem, []

    def add(self, src, dst):
        c = pltpu.make_async_copy(src, dst, self.sem)
        c.start()
        self.list.append(c)

    def halves(self, src, dst):
        n = len(src.shape) - 2
        for h in range(2):
            full = (slice(None),) * n
            self.add(
                src.at[full + (slice(None), pl.ds(LANES * h, LANES))],
                dst.at[full + (h, pl.ds(8, CY), slice(None))],
            )

    def halves_out(self, src, dst):
        n = len(dst.shape) - 2
        for h in range(2):
            full = (slice(None),) * n
            self.add(
                src.at[full + (h, pl.ds(8, CY), slice(None))],
                dst.at[full + (slice(None), pl.ds(LANES * h, LANES))],
            )

    def wait(self):
        for c in self.list:
            c.wait()
        self.list = []


def clear_pads(f, first, last):
    zero = jnp.zeros((8, LANES), F32)

    @pl.loop(first, last)
    def _(x):
        for v in range(NV):
            for h in range(2):
                f[v, x, h, 0:8, :] = zero
                f[v, x, h, PADY - 8 : PADY, :] = zero


def tile_terms(f, x, t, jh, kap):
    lane = lax.broadcasted_iota(I32, (8, LANES), 1)
    y0 = pl.multiple_of(8 * t + 8, 8)
    acc = [[None, None] for _ in range(NV)]
    centres = []
    for w in range(NV):
        c = [f[w, x, h, pl.ds(y0, 8), :] for h in range(2)]
        down = [pltpu.roll(c[h], 1, 1) for h in range(2)]
        up = [pltpu.roll(c[h], LANES - 1, 1) for h in range(2)]
        zm = [jnp.where(lane == 0, 0.0, down[0]), jnp.where(lane == 0, down[0], down[1])]
        zp = [
            jnp.where(lane == LANES - 1, up[1], up[0]),
            jnp.where(lane == LANES - 1, 0.0, up[1]),
        ]
        for h in range(2):
            xm, xp = f[w, x - 1, h, pl.ds(y0, 8), :], f[w, x + 1, h, pl.ds(y0, 8), :]
            ym, yp = f[w, x, h, pl.ds(y0 - 1, 8), :], f[w, x, h, pl.ds(y0 + 1, 8), :]
            dx, dy, dz = xp - xm, yp - ym, zp[h] - zm[h]
            beside = (xp + xm) + (yp + ym) + (zp[h] + zm[h])
            for v in range(NV):
                term = jh[v * 6 + w] * dx + jh[36 + v * 6 + w] * dy + jh[72 + v * 6 + w] * dz
                if v == w:
                    term = term - kap[h] * beside
                acc[v][h] = term if acc[v][h] is None else acc[v][h] + term
        centres.append(c)
    return acc, centres


def kap_tile(kap, k, t):
    y0 = pl.multiple_of(8 * t, 8)
    both = [kap[k, pl.ds(y0, 8), half_of(h)] for h in range(2)]
    return both, [-1.0 / (PSEUDO_DIAG + 6.0 * b) for b in both]


def each_tile(count, row_of, body):
    @pl.loop(0, count * (NT // 2))
    def _(n):
        i = n // (NT // 2)
        row = row_of(i)
        for u in range(2):
            body(i, row, 2 * (n % (NT // 2)) + u)


def start_row(f, at, kap, k, now, prev, n, t, jh, emit):
    kp, ninv = kap_tile(kap, k, t)
    acc, centres = tile_terms(f, at, t, jh, kp)
    y0 = pl.multiple_of(8 * t, 8)
    for v in range(NV):
        for h in range(2):
            c = centres[v][h]
            past = prev[v, n, pl.ds(y0, 8), half_of(h)]
            if now is None:
                own = 0.5 * (past - c)
            else:
                own = 0.5 * (3.0 * c + (past - 4.0 * now[v, n, pl.ds(y0, 8), half_of(h)]))
            r = own + acc[v][h] + (6.0 * kp[h]) * c
            emit(v, h, r, r * ninv[h])


def relax_row(f, at, rs, ra, kap, k, t, jh, emit):
    kp, ninv = kap_tile(kap, k, t)
    acc, _ = tile_terms(f, at, t, jh, kp)
    y0 = pl.multiple_of(8 * t, 8)
    for v in range(NV):
        for h in range(2):
            emit(v, h, (rs[v, ra, pl.ds(y0, 8), half_of(h)] + acc[v][h]) * ninv[h])


def edge_rows(side, f, kap, now, prev, jh, ers, es1):
    def body(i, row, t):
        y0 = pl.multiple_of(8 * t, 8)
        at = i + 2 * side

        def emit(v, h, r, s):
            ers[v, at, pl.ds(y0, 8), half_of(h)] = r
            es1[v, at, pl.ds(y0, 8), half_of(h)] = s

        start_row(f, row + 1, kap, at, now, prev, at, t, jh, emit)

    each_tile(2, lambda i: i + 6 * side, body)


def edge_load(c, side, now, prev, kap, nowb, prevb, kapb):
    x, i = 6 * side, 2 * side
    if nowb is not None:
        c.add(now.at[:, pl.ds(x, 2)], nowb.at[:, pl.ds(i, 2)])
    c.add(prev.at[:, pl.ds(x, 2)], prevb.at[:, pl.ds(i, 2)])
    c.add(kap.at[pl.ds(x, 2)], kapb.at[pl.ds(i, 2)])


def edge_send(c, side, f, kap, ers, es1, msg, er):
    outer, inner = 3 * side, 1 + side
    c.halves_out(f.at[:, 1 + (CX - 1) * side], msg.at[pl.ds(0, NV)])
    c.add(ers.at[:, outer], msg.at[pl.ds(NV, NV)])
    c.add(es1.at[:, inner], msg.at[pl.ds(2 * NV, NV)])
    if msg.shape[0] > 3 * NV:
        c.add(kap.at[outer], msg.at[3 * NV])
    c.add(ers.at[:, inner], er.at[:, side])


def edge_zero(f):
    @pl.loop(0, CY // 8)
    def _(t):
        for v in range(NV):
            for h in range(2):
                for x in (0, CX + 1):
                    f[v, x, h, pl.ds(pl.multiple_of(8 * t + 8, 8), 8), :] = jnp.zeros((8, LANES), F32)


EDGE_SCRATCH = (
    pltpu.VMEM((NV, 4, CY, CZ), F32), pltpu.VMEM((NV, 4, CY, CZ), F32), pltpu.VMEM((4, CY, CZ), F32),
    pltpu.VMEM((NV, 4, CY, CZ), F32), pltpu.VMEM((NV, 4, CY, CZ), F32),
)


def edge_body(now, prev, kap, jh, lo, hi, er, f, nowb, prevb, kapb, ers, es1, sem):
    groups = []
    for side in range(2):
        c = Copies(sem.at[side])
        c.halves(now.at[:, pl.ds(5 * side, 3)], f.at[:, pl.ds(5 * side + 1, 3)])
        edge_load(c, side, now, prev, kap, None, prevb, kapb)
        groups.append(c)
    clear_pads(f, 1, 4)
    clear_pads(f, 6, 9)
    edge_zero(f)
    for side, msg in ((0, lo), (1, hi)):
        groups[side].wait()
        edge_rows(side, f, kapb, None, prevb, jh, ers, es1)
        edge_send(groups[side], side, f, kapb, ers, es1, msg, er)
    for c in groups:
        c.wait()


def inner_body(
    q, now, prev, kap, jh, lo, hi, rs_out, s1_out, s2_out, s3_out,
    f, nowb, prevb, kapb, rs, s1, s2, s3, sem, later=True,
):
    groups = []
    for k, x, n in ((0, 1, 4), (1, 5, 2)):
        c = Copies(sem.at[k])
        c.halves(q.at[:, pl.ds(x, n)], f.at[:, pl.ds(x - 1, n)])
        rows = pl.ds(2 + 2 * k, 2)
        if later:
            c.add(now.at[:, rows], nowb.at[:, pl.ds(2 * k, 2)])
        c.add(prev.at[:, rows], prevb.at[:, pl.ds(2 * k, 2)])
        c.add(kap.at[rows], kapb.at[pl.ds(2 * k, 2)])
        groups.append(c)
    c = groups[1]
    c.halves(lo.at[pl.ds(2 * NV, NV)], s1.at[:, 0])
    c.halves(hi.at[pl.ds(2 * NV, NV)], s1.at[:, 5])
    clear_pads(f, 1, 5)
    clear_pads(s1, 1, 5)
    clear_pads(s2, 1, 3)

    def first(i, row, t):
        def emit(v, h, r, s):
            rs[v, row, pl.ds(pl.multiple_of(8 * t, 8), 8), half_of(h)] = r
            s1[v, row + 1, h, pl.ds(pl.multiple_of(8 * t + 8, 8), 8), :] = s

        start_row(f, row + 1, kapb, row, nowb if later else None, prevb, row, t, jh, emit)

    groups[0].wait()
    each_tile(2, lambda i: i, first)
    groups[1].wait()
    each_tile(2, lambda i: i + 2, first)
    for i in range(2):
        c.add(rs.at[:, 3 * i], rs_out.at[:, i])
        c.halves_out(s1.at[:, 3 * i + 1], s1_out.at[:, i])

    def second(i, row, t):
        def emit(v, h, val):
            s2[v, i, h, pl.ds(pl.multiple_of(8 * t + 8, 8), 8), :] = val

        relax_row(s1, i + 1, rs, i, kapb, i, t, jh, emit)

    each_tile(4, lambda i: i, second)
    c.halves_out(s2, s2_out)

    def third(i, row, t):
        def emit(v, h, val):
            s3[v, i, pl.ds(pl.multiple_of(8 * t, 8), 8), half_of(h)] = val

        relax_row(s2, i + 1, rs, i + 1, kapb, i + 1, t, jh, emit)

    each_tile(2, lambda i: i, third)
    c.add(s3, s3_out)
    c.wait()


INNER_SCRATCH = (
    field(6), pltpu.VMEM((NV, 4, CY, CZ), F32), pltpu.VMEM((NV, 4, CY, CZ), F32), pltpu.VMEM((4, CY, CZ), F32),
    pltpu.VMEM((NV, 4, CY, CZ), F32), field(6), field(4), pltpu.VMEM((NV, 2, CY, CZ), F32), pltpu.SemaphoreType.DMA((2,)),
)


def fix_rows(rse, s1e, far, kape, jh, lo_ok, hi_ok):
    def body(i, row, t):
        y0 = pl.multiple_of(8 * t, 8)
        sign = jnp.where(i % 2 == 0, 1.0, -1.0).astype(F32)
        scale = jnp.where(i == 0, lo_ok, jnp.where(i == 3, hi_ok, 1.0))
        kp, ninv = kap_tile(kape, row + 1, t)
        for h in range(2):
            side = [far[w, i, pl.ds(y0, 8), half_of(h)] for w in range(NV)]
            turned = [side[w] * sign for w in range(NV)]
            for v in range(NV):
                r = rse[v, row + 1, pl.ds(y0, 8), half_of(h)] - kp[h] * side[v]
                for w in range(NV):
                    r = r + jh[v * 6 + w] * turned[w]
                rse[v, row + 1, pl.ds(y0, 8), half_of(h)] = r
                s1e[v, row + 2, h, pl.ds(pl.multiple_of(y0 + 8, 8), 8), :] = r * (ninv[h] * scale)

    each_tile(4, lambda i: i - 1 + 6 * (i // 2), body)


def finish_body(
    q, kap, jh, who, idx_in, pairs_in, own_lo, own_hi, got_lo, got_hi, klo, khi, w_in,
    er, rs_in, s1_in, s2_in, s3_in, qn, send,
    rse, s1e, s2e, kape, far, qb, s3, q8, tab, g, wb, idx, pairs, sem,
):
    lo_ok = jnp.where(who[1] > 0, 1.0, 0.0).astype(F32)
    hi_ok = jnp.where(who[1] < who[2] - 1, 1.0, 0.0).astype(F32)
    c, d, e, k = (Copies(sem.at[n]) for n in range(4))
    for i, msg in ((0, own_lo), (1, got_lo), (2, got_hi), (3, own_hi)):
        c.add(msg.at[pl.ds(0, NV)], far.at[:, i])
    for x, msg in ((0, got_lo), (1, own_lo), (8, own_hi), (9, got_hi)):
        c.add(msg.at[pl.ds(NV, NV)], rse.at[:, x])
    c.add(kap, kape.at[pl.ds(1, CX)])
    c.add(klo.at[3 * NV], kape.at[0])
    c.add(khi.at[3 * NV], kape.at[CX + 1])
    for x, msg in ((0, got_lo), (3, own_lo), (8, own_hi), (11, got_hi)):
        k.halves(msg.at[pl.ds(2 * NV, NV)], s1e.at[:, x])
    for i, (r, s) in enumerate(((2, 4), (7, 7))):
        k.add(er.at[:, i], rse.at[:, r])
        k.add(rs_in.at[:, i], rse.at[:, (3, 6)[i]])
        k.halves(s1_in.at[:, i], s1e.at[:, s])
    d.halves(s2_in, s2e.at[:, pl.ds(3, 4)])
    d.add(q, qb)
    d.add(s3_in, s3)
    e.add(w_in, wb)
    e.add(idx_in, idx)
    e.add(pairs_in, pairs)
    clear_pads(s1e, 1, 4)
    clear_pads(s1e, 8, 11)
    clear_pads(s2e, 1, 4)
    clear_pads(s2e, 6, 9)
    c.wait()

    fix_rows(rse, s1e, far, kape, jh, lo_ok, hi_ok)
    k.wait()

    def second(i, row, t):
        scale = jnp.where(i == 0, lo_ok, jnp.where(i == 5, hi_ok, 1.0))

        def emit(v, h, val):
            s2e[v, row + 1, h, pl.ds(pl.multiple_of(8 * t + 8, 8), 8), :] = val * scale

        relax_row(s1e, row + 2, rse, row + 1, kape, row + 1, t, jh, emit)

    each_tile(6, lambda i: i - 1 + 4 * (i // 3), second)
    d.wait()

    def put(row, v, h, t, val):
        qb[v, row, pl.ds(pl.multiple_of(8 * t, 8), 8), half_of(h)] = val
        q8[row, h, pl.ds(64 * t + v, 8, stride=8), :] = val

    def third(i, row, t):
        def emit(v, h, val):
            put(row, v, h, t, qb[v, row, pl.ds(pl.multiple_of(8 * t, 8), 8), half_of(h)] + val)

        relax_row(s2e, row + 1, rse, row + 1, kape, row + 1, t, jh, emit)

    each_tile(6, lambda i: i + 2 * (i // 3), third)

    def rest(i, row, t):
        y0 = pl.multiple_of(8 * t, 8)
        for v in range(NV):
            for h in range(2):
                put(row, v, h, t, qb[v, row, pl.ds(y0, 8), half_of(h)] + s3[v, i, pl.ds(y0, 8), half_of(h)])

    each_tile(2, lambda i: i + 3, rest)
    d.add(qb, qn)
    gather_points(idx, pairs, who[0], wb, e, send, q8, tab, g)
    d.wait()


FINISH_SCRATCH = (
    pltpu.VMEM((NV, CX + 2, CY, CZ), F32), field(CX + 4), field(CX + 2), pltpu.VMEM((CX + 2, CY, CZ), F32),
    pltpu.VMEM((NV, 4, CY, CZ), F32), pltpu.VMEM((NV, CX, CY, CZ), F32), pltpu.VMEM((NV, 2, CY, CZ), F32),
    pltpu.VMEM((CX, 2, 8 * CY, LANES), F32),
    pltpu.VMEM((DONOR_ROWS + 8, LANES), F32),
    pltpu.VMEM((2 * POINTS, LANES), F32),
    pltpu.VMEM((2, POINTS, LANES), F32),
    pltpu.SMEM((POINTS,), I32),
    pltpu.SMEM((16, 16), I32),
    pltpu.SemaphoreType.DMA((4,)),
)


def gather_points(idx, pairs, me, wb, loads, send, q8, tab, g):
    @pl.loop(0, YGROUPS)
    def _(yg):
        first = pl.multiple_of(jnp.minimum(yg * 3, CY - 4) * 8, 8)
        for xg in range(2):
            for h in range(2):
                block = [q8[xg * 3 + xx, h, pl.ds(first, 32), :] for xx in range(4)]
                row = pl.multiple_of((xg * YGROUPS + yg) * CZ + h * LANES, LANES)
                tab[pl.ds(row, LANES), :] = jnp.concatenate(block, axis=0).T

    loads.wait()

    @pl.loop(0, TILES)
    def _(tile):
        @pl.when(tile % 2 < pairs[me, tile // 2])
        def _():
            for u in range(LANES):
                row = idx[pl.multiple_of(tile * LANES, LANES) + u]
                at = pl.multiple_of(tile * 2 * LANES, 2 * LANES) + 2 * u
                g[pl.ds(at, 2), :] = tab[pl.ds(row, 2), :]

    @pl.loop(0, TILES // 8)
    def _(n):
        for u in range(8):
            o = pl.multiple_of(n * 8 * LANES + u * LANES, LANES)
            here = g[pl.ds(o * 2, LANES, stride=2), :] * wb[0, pl.ds(o, LANES), :]
            here = here + g[pl.ds(o * 2 + 1, LANES, stride=2), :] * wb[1, pl.ds(o, LANES), :]
            turned = here.T
            parts = [turned[8 * k : 8 * k + 8] for k in range(16)]
            while len(parts) > 1:
                parts = [a + b for a, b in zip(parts[::2], parts[1::2])]
            send[4 * n + u // 2, u % 2] = parts[0]


def setup_body(
    donor_in, recv_in, pairs_in, who, held_in, didx_out, ridx_out, w_out,
    donor, recv, pairs, held, didx, dpos, ridx, w, sem,
):
    c = Copies(sem.at[0])
    c.add(donor_in, donor)
    c.add(recv_in, recv)
    c.add(pairs_in, pairs)
    d = Copies(sem.at[1])
    d.add(held_in, held)
    c.wait()
    me = who[0]
    for s in range(16):
        live = pairs[s, me]
        for t in range(2):
            i = 2 * s + t
            cell = donor[s, t, 0:1, :]
            x, y, z = cell >> 13, (cell >> 8) & (CY - 1), cell & (CZ - 1)
            xg = jnp.where(x >= 3, 1, 0)
            yg = (y * 11) >> 5
            didx[i : i + 1, :] = (xg * YGROUPS + yg) * CZ + z
            dpos[i : i + 1, :] = (x - 3 * xg) * 4 + (y - jnp.minimum(yg * 3, CY - 4))
            cell = recv[s, t : t + 1, :]
            x, y, z = cell >> 13, (cell >> 8) & (CY - 1), cell & (CZ - 1)
            row = (2 * x + (y >> 4)) * CZ + z
            row = jnp.where(t < live, row, RECV_ROWS)
            ridx[i : i + 1, :] = row * 16 + (y & 15)
    c.add(didx, didx_out)
    c.add(ridx, ridx_out)
    d.wait()

    def weigh(tile, u):
        kpos = lax.broadcasted_iota(I32, (16, LANES), 0)
        base = jnp.broadcast_to(dpos[pl.ds(tile, 1), :], (16, LANES))
        o = pl.multiple_of(tile * LANES, LANES)
        for l in range(2):
            grid = jnp.zeros((16, LANES), F32)
            for i in range(2):
                for j in range(2):
                    k = 4 * i + 2 * j + l
                    row = jnp.broadcast_to(held[tile // 2, u, k : k + 1, :], (16, LANES))
                    grid = jnp.where(kpos == base + (4 * i + j), row, grid)
            wide = [jnp.broadcast_to(grid[k : k + 1], (8, LANES)) for k in range(16)]
            w[l, pl.ds(o, LANES), :] = jnp.concatenate(wide, axis=0).T

    for part in range(4):

        @pl.loop(0, TILES // 16)
        def _(m):
            for u in range(4):
                weigh(part * (TILES // 4) + 4 * m + u, u % 2)

        rows = pl.ds(part * (POINTS // 4), POINTS // 4)
        d.add(w.at[:, rows], w_out.at[:, rows])
    c.wait()
    d.wait()


SETUP_SCRATCH = (
    pltpu.VMEM((16, 2, 8, LANES), I32),
    pltpu.VMEM((16, 2, LANES), I32),
    pltpu.SMEM((16, 16), I32),
    pltpu.VMEM((16, 2, 8, LANES), F32),
    pltpu.VMEM((TILES, LANES), I32),
    pltpu.VMEM((TILES, LANES), I32),
    pltpu.VMEM((TILES, LANES), I32),
    pltpu.VMEM((2, POINTS, LANES), F32),
    pltpu.SemaphoreType.DMA((2,)),
)


def scatter_points(vals, ridx, qb, arrive, loads, write, vrep, u, ut, half=None):
    mark = lax.broadcasted_iota(I32, (8, LANES), 0) == NV
    lane = lax.broadcasted_iota(I32, (1, LANES), 1) >> 3

    @pl.loop(0, RECV_ROWS // LANES)
    def _(i):
        u[pl.ds(pl.multiple_of(i * LANES, LANES), LANES), :] = jnp.zeros((LANES, LANES), F32)

    @pl.loop(0, TILES // 8)
    def _(n):
        for k in range(8):
            v = jnp.where(mark, 1.0, vals[4 * n + k // 2, k % 2])
            rows = pl.ds(pl.multiple_of(n * 8 * LANES + k * LANES, LANES), LANES)
            vrep[rows, :] = jnp.concatenate([v] * 16, axis=0).T

    loads.wait()

    @pl.loop(0, POINTS // 64)
    def _(b):
        for j in range(64):
            at = pl.multiple_of(b * 64, 64) + j
            word = ridx[at]
            mask = (jnp.full((1, LANES), word, I32) & 15) == lane
            pltpu.store(u.at[pl.ds(word >> 4, 1), :], vrep[pl.ds(at, 1), :], mask=mask)

    @pl.loop(0, CX - 1)
    def _(x):
        for yh in range(2):
            for h in range(2):
                row = pl.multiple_of((2 * x + yh) * CZ + h * LANES, LANES)
                ut[2 * x + yh, h] = u[pl.ds(row, LANES), :].T

    arrive.wait()

    def merge(x):
        for yh in range(2):
            for h in range(2):
                for t in range(2):
                    part = ut.at[2 * x + yh, h]
                    hit = part[pl.ds(64 * t + NV, 8, stride=8), :] != 0.0
                    y = 16 * yh + 8 * t
                    for v in range(NV):
                        new = part[pl.ds(64 * t + v, 8, stride=8), :]
                        old = qb[v, x, y : y + 8, half_of(h)]
                        write(v, x, h, y, jnp.where(hit, new, old))

    pl.loop(0, 4)(merge)
    if half is not None:
        half()
    pl.loop(4, CX - 1)(merge)


def scatter_body(q, vals, ridx_in, out, qb, vrep, u, ut, ridx, sem):
    c, e = Copies(sem.at[0]), Copies(sem.at[2])
    e.add(ridx_in, ridx)
    c.add(q, qb)

    def write(v, x, h, y, val):
        qb[v, x, y : y + 8, half_of(h)] = val

    def half():
        c.add(qb.at[:, pl.ds(0, 4)], out.at[:, pl.ds(0, 4)])

    scatter_points(vals, ridx, qb, c, e, write, vrep, u, ut, half)
    c.add(qb.at[:, pl.ds(4, 4)], out.at[:, pl.ds(4, 4)])
    c.wait()


def scatter_edge_body(
    q, vals, ridx_in, now, prev, kap, jh, out, lo, hi, er,
    qb, vrep, u, ut, ridx, f, nowb, prevb, kapb, ers, es1, sem,
):
    c, e = Copies(sem.at[0]), Copies(sem.at[2])
    e.add(ridx_in, ridx)
    c.add(q, qb)
    d = Copies(sem.at[1])
    for side in range(2):
        edge_load(d, side, now, prev, kap, nowb, prevb, kapb)
    clear_pads(f, 1, 4)
    clear_pads(f, 6, 9)
    edge_zero(f)

    def write(v, x, h, y, val):
        f[v, x + 1, h, 8 + y : 16 + y, :] = val

    scatter_points(vals, ridx, qb, c, e, write, vrep, u, ut)
    for v in range(NV):
        for h in range(2):
            f[v, CX, h, 8 : 8 + CY, :] = qb[v, CX - 1, :, half_of(h)]
    c.halves_out(f.at[:, pl.ds(1, CX)], out)
    d.wait()
    for side, msg in ((0, lo), (1, hi)):
        edge_rows(side, f, kapb, nowb, prevb, jh, ers, es1)
        edge_send(d, side, f, kapb, ers, es1, msg, er)
    d.wait()
    c.wait()


STATE = (NV, CX, CY, CZ)
SCATTER_SCRATCH = (
    pltpu.VMEM((NV, CX, CY, CZ), F32),
    pltpu.VMEM((POINTS, LANES), F32),
    pltpu.VMEM((RECV_ROWS + 8, LANES), F32),
    pltpu.VMEM((RECV_GROUPS, 2, LANES, LANES), F32),
    pltpu.SMEM((POINTS,), I32),
)


def rows_of(n):
    return sds((NV, n, CY, CZ))


def shards(
    state_now, state_prev, viscosity, jacobian, donor_cell, interp_weight, recv_cell, pair_tiles
):
    now = state_now[0]
    prev = state_prev[0]
    kap = viscosity[0]
    jh = (jacobian[0] * 0.5).reshape(-1)
    count = lax.axis_size("blk")
    at = lax.axis_index("blk")
    me = lax.axis_index("comp")
    who = jnp.stack([me, at, jnp.int32(count)]).astype(I32)
    pairs = pair_tiles[0]
    forward = [(i, i + 1) for i in range(count - 1)]
    backward = [(b, a) for a, b in forward]

    def messages(planes):
        return [sds((planes, CY, CZ))] * 2 + [rows_of(2)]


    idx_shape = sds((TILES, LANES), I32)
    sems = pltpu.SemaphoreType.DMA((3,))

    lo, hi, er = call(
        edge_body, "edge", messages(3 * NV + 1), [HBM] * 3 + [SMEM], [HBM] * 3,
        scratch=(field(CX + 2),) + EDGE_SCRATCH + (sems,), cost_us=3.0,
    )(now, prev, kap, jh)
    state = now
    for sub in range(2):
        kept = HBM if sub == 0 else ANY
        got_lo = lax.ppermute(hi, "blk", forward)
        got_hi = lax.ppermute(lo, "blk", backward)
        if sub == 0:
            klo, khi = got_lo, got_hi
        inner = call(
            functools.partial(inner_body, later=sub > 0), "inner", [rows_of(n) for n in (2, 2, 4, 2)],
            [kept, HBM, HBM, HBM, SMEM, kept, kept], [kept] * 4,
            scratch=INNER_SCRATCH, vmem_mb=14, cost_us=4.0,
        )(state, now, prev, kap, jh, lo, hi)
        if sub == 0:
            weights, _ = lax.optimization_barrier((interp_weight[0, 0], lo))
            held = lax.all_to_all(weights, "comp", split_axis=0, concat_axis=0, tiled=True)
            didx, ridx, wide = call(
                setup_body, "setup", [idx_shape] * 2 + [sds((2, POINTS, LANES))],
                [HBM] * 3 + [SMEM, ANY], [HBM] * 3, scratch=SETUP_SCRATCH, cost_us=4.0,
            )(donor_cell[0, 0], recv_cell[0, 0], pairs, who, held)
            didx, ridx = didx.reshape(-1), ridx.reshape(-1)
        relaxed, send = call(
            finish_body, "finish", [sds(STATE), sds((16, 2, 8, LANES))],
            [kept, HBM, SMEM, SMEM, HBM, HBM, kept, kept, ANY, ANY, ANY, ANY, HBM] + [kept] * 5,
            [ANY, VMEM], scratch=FINISH_SCRATCH, vmem_mb=30, cost_us=14.0,
        )(
            state, kap, jh, who, didx, pairs, lo, hi, got_lo, got_hi, klo, khi, wide,
            er, *inner,
        )
        arrived = lax.all_to_all(send, "comp", split_axis=0, concat_axis=0, tiled=True)
        if sub == 0:
            state, lo, hi, er = call(
                scatter_edge_body, "scatter_edge", [sds(STATE)] + messages(3 * NV),
                [ANY, VMEM, HBM, HBM, HBM, HBM, SMEM], [ANY] * 4,
                scratch=SCATTER_SCRATCH + (field(CX + 2),) + EDGE_SCRATCH + (sems,),
                vmem_mb=20, cost_us=12.0,
            )(relaxed, arrived, ridx, now, prev, kap, jh)
        else:
            state = call(
                scatter_body, "scatter", sds(STATE), [ANY, VMEM, HBM], HBM,
                scratch=SCATTER_SCRATCH + (sems,), vmem_mb=12, cost_us=10.0,
            )(relaxed, arrived, ridx)
    return state[None]


def solution(mesh):
    in_specs = (
        P("comp", None, "blk", None, None),
        P("comp", None, "blk", None, None),
        P("comp", "blk", None, None),
        P("comp", None, None, None),
        P("comp", "blk", None, None, None, None),
        P("comp", "blk", None, None, None, None),
        P("comp", "blk", None, None, None),
        P("blk", None, None),
    )
    out_specs = P("comp", None, "blk", None, None)
    return jax.shard_map(shards, mesh=mesh, in_specs=in_specs, out_specs=out_specs, check_vma=False)
```

```python
import functools

import jax
import jax.numpy as jnp
from jax import lax
from jax.experimental import pallas as pl
from jax.experimental.pallas import tpu as pltpu
from jax.sharding import PartitionSpec as P

F32 = jnp.float32
I32 = jnp.int32
NV, CX, CY, CZ = 6, 8, 32, 256
LANES = 128
TILES = 32
POINTS = TILES * LANES
NT = CY // 8
YGROUPS = 11
DONOR_ROWS = 2 * YGROUPS * CZ
RECV_GROUPS = 2 * (CX - 1)
RECV_ROWS = RECV_GROUPS * CZ
PSEUDO_DIAG = 2.5
VMEM = pl.BlockSpec(memory_space=pltpu.VMEM)
SMEM = pl.BlockSpec(memory_space=pltpu.SMEM)
HBM = pl.BlockSpec(memory_space=pltpu.HBM)
ANY = pl.BlockSpec(memory_space=pl.ANY)
PADY = CY + 16
HALF = CZ // 2


def sds(shape, dtype=F32):
    return jax.ShapeDtypeStruct(shape, dtype)


def field(rows):
    return pltpu.VMEM((NV, rows, 2, PADY, LANES), F32)


def half_of(h):
    return pl.ds(LANES * h, LANES)


def call(body, name, outs, ins, out_specs, scratch=(), vmem_mb=12, cost_us=1.0):
    outs = jax.tree.map(
        lambda o, spec: pltpu.HBM(o.shape, o.dtype) if spec is HBM else o, outs, out_specs
    )
    kernel = pl.pallas_call(
        body,
        out_shape=outs,
        in_specs=ins,
        out_specs=out_specs,
        scratch_shapes=list(scratch),
        compiler_params=pltpu.CompilerParams(vmem_limit_bytes=vmem_mb << 20),
        cost_estimate=pl.CostEstimate(
            flops=0, transcendentals=0, bytes_accessed=int(cost_us * 3.0e6)
        ),
        name=name,
    )

    def run(*args):
        return kernel(*[
            pltpu.with_memory_space_constraint(a, pltpu.HBM) if spec is HBM else a
            for a, spec in zip(args, ins, strict=True)
        ])

    return run


class Copies:
    def __init__(self, sem):
        self.sem, self.list = sem, []

    def add(self, src, dst):
        c = pltpu.make_async_copy(src, dst, self.sem)
        c.start()
        self.list.append(c)

    def halves(self, src, dst):
        n = len(src.shape) - 2
        for h in range(2):
            full = (slice(None),) * n
            self.add(
                src.at[full + (slice(None), pl.ds(LANES * h, LANES))],
                dst.at[full + (h, pl.ds(8, CY), slice(None))],
            )

    def halves_out(self, src, dst):
        n = len(dst.shape) - 2
        for h in range(2):
            full = (slice(None),) * n
            self.add(
                src.at[full + (h, pl.ds(8, CY), slice(None))],
                dst.at[full + (slice(None), pl.ds(LANES * h, LANES))],
            )

    def wait(self):
        for c in self.list:
            c.wait()
        self.list = []


def clear_pads(f, first, last):
    zero = jnp.zeros((8, LANES), F32)

    @pl.loop(first, last)
    def _(x):
        for v in range(NV):
            for h in range(2):
                f[v, x, h, 0:8, :] = zero
                f[v, x, h, PADY - 8 : PADY, :] = zero


def tile_terms(f, x, t, jh, kap):
    lane = lax.broadcasted_iota(I32, (8, LANES), 1)
    y0 = pl.multiple_of(8 * t + 8, 8)
    acc = [[None, None] for _ in range(NV)]
    centres = []
    for w in range(NV):
        c = [f[w, x, h, pl.ds(y0, 8), :] for h in range(2)]
        down = [pltpu.roll(c[h], 1, 1) for h in range(2)]
        up = [pltpu.roll(c[h], LANES - 1, 1) for h in range(2)]
        zm = [jnp.where(lane == 0, 0.0, down[0]), jnp.where(lane == 0, down[0], down[1])]
        zp = [
            jnp.where(lane == LANES - 1, up[1], up[0]),
            jnp.where(lane == LANES - 1, 0.0, up[1]),
        ]
        for h in range(2):
            xm, xp = f[w, x - 1, h, pl.ds(y0, 8), :], f[w, x + 1, h, pl.ds(y0, 8), :]
            ym, yp = f[w, x, h, pl.ds(y0 - 1, 8), :], f[w, x, h, pl.ds(y0 + 1, 8), :]
            dx, dy, dz = xp - xm, yp - ym, zp[h] - zm[h]
            beside = (xp + xm) + (yp + ym) + (zp[h] + zm[h])
            for v in range(NV):
                term = jh[v * 6 + w] * dx + jh[36 + v * 6 + w] * dy + jh[72 + v * 6 + w] * dz
                if v == w:
                    term = term - kap[h] * beside
                acc[v][h] = term if acc[v][h] is None else acc[v][h] + term
        centres.append(c)
    return acc, centres


def kap_tile(kap, k, t):
    y0 = pl.multiple_of(8 * t, 8)
    both = [kap[k, pl.ds(y0, 8), half_of(h)] for h in range(2)]
    return both, [-1.0 / (PSEUDO_DIAG + 6.0 * b) for b in both]


def each_tile(count, row_of, body):
    @pl.loop(0, count)
    def _(i):
        row = row_of(i)
        for t in range(NT):
            body(i, row, t)


def start_row(f, at, kap, k, now, prev, n, t, jh, emit):
    kp, ninv = kap_tile(kap, k, t)
    acc, centres = tile_terms(f, at, t, jh, kp)
    y0 = pl.multiple_of(8 * t, 8)
    for v in range(NV):
        for h in range(2):
            c = centres[v][h]
            past = prev[v, n, pl.ds(y0, 8), half_of(h)]
            if now is None:
                own = 0.5 * (past - c)
            else:
                own = 0.5 * (3.0 * c + (past - 4.0 * now[v, n, pl.ds(y0, 8), half_of(h)]))
            r = own + acc[v][h] + (6.0 * kp[h]) * c
            emit(v, h, r, r * ninv[h])


def relax_row(f, at, rs, ra, kap, k, t, jh, emit):
    kp, ninv = kap_tile(kap, k, t)
    acc, _ = tile_terms(f, at, t, jh, kp)
    y0 = pl.multiple_of(8 * t, 8)
    for v in range(NV):
        for h in range(2):
            emit(v, h, (rs[v, ra, pl.ds(y0, 8), half_of(h)] + acc[v][h]) * ninv[h])


def edge_rows(side, f, kap, now, prev, jh, ers, es1):
    def body(i, row, t):
        y0 = pl.multiple_of(8 * t, 8)
        at = i + 2 * side

        def emit(v, h, r, s):
            ers[v, at, pl.ds(y0, 8), half_of(h)] = r
            es1[v, at, pl.ds(y0, 8), half_of(h)] = s

        start_row(f, row + 1, kap, at, now, prev, at, t, jh, emit)

    each_tile(2, lambda i: i + 6 * side, body)


def edge_load(c, side, now, prev, kap, nowb, prevb, kapb):
    x, i = 6 * side, 2 * side
    if nowb is not None:
        c.add(now.at[:, pl.ds(x, 2)], nowb.at[:, pl.ds(i, 2)])
    c.add(prev.at[:, pl.ds(x, 2)], prevb.at[:, pl.ds(i, 2)])
    c.add(kap.at[pl.ds(x, 2)], kapb.at[pl.ds(i, 2)])


def edge_send(c, side, f, kap, ers, es1, msg, er):
    outer, inner = 3 * side, 1 + side
    c.halves_out(f.at[:, 1 + (CX - 1) * side], msg.at[pl.ds(0, NV)])
    c.add(ers.at[:, outer], msg.at[pl.ds(NV, NV)])
    c.add(es1.at[:, inner], msg.at[pl.ds(2 * NV, NV)])
    if msg.shape[0] > 3 * NV:
        c.add(kap.at[outer], msg.at[3 * NV])
    c.add(ers.at[:, inner], er.at[:, side])


def edge_zero(f):
    @pl.loop(0, CY // 8)
    def _(t):
        for v in range(NV):
            for h in range(2):
                for x in (0, CX + 1):
                    f[v, x, h, pl.ds(pl.multiple_of(8 * t + 8, 8), 8), :] = jnp.zeros((8, LANES), F32)


EDGE_SCRATCH = (
    pltpu.VMEM((NV, 4, CY, CZ), F32), pltpu.VMEM((NV, 4, CY, CZ), F32), pltpu.VMEM((4, CY, CZ), F32),
    pltpu.VMEM((NV, 4, CY, CZ), F32), pltpu.VMEM((NV, 4, CY, CZ), F32),
)


def edge_body(now, prev, kap, jh, lo, hi, er, f, nowb, prevb, kapb, ers, es1, sem):
    groups = []
    for side in range(2):
        c = Copies(sem.at[side])
        c.halves(now.at[:, pl.ds(5 * side, 3)], f.at[:, pl.ds(5 * side + 1, 3)])
        edge_load(c, side, now, prev, kap, None, prevb, kapb)
        groups.append(c)
    clear_pads(f, 1, 4)
    clear_pads(f, 6, 9)
    edge_zero(f)
    for side, msg in ((0, lo), (1, hi)):
        groups[side].wait()
        edge_rows(side, f, kapb, None, prevb, jh, ers, es1)
        edge_send(groups[side], side, f, kapb, ers, es1, msg, er)
    for c in groups:
        c.wait()


def inner_body(
    q, now, prev, kap, jh, lo, hi, rs_out, s1_out, s2_out, s3_out,
    f, nowb, prevb, kapb, rs, s1, s2, s3, sem, later=True,
):
    groups = []
    for k, x, n in ((0, 1, 4), (1, 5, 2)):
        c = Copies(sem.at[k])
        c.halves(q.at[:, pl.ds(x, n)], f.at[:, pl.ds(x - 1, n)])
        rows = pl.ds(2 + 2 * k, 2)
        if later:
            c.add(now.at[:, rows], nowb.at[:, pl.ds(2 * k, 2)])
        c.add(prev.at[:, rows], prevb.at[:, pl.ds(2 * k, 2)])
        c.add(kap.at[rows], kapb.at[pl.ds(2 * k, 2)])
        groups.append(c)
    c = groups[1]
    c.halves(lo.at[pl.ds(2 * NV, NV)], s1.at[:, 0])
    c.halves(hi.at[pl.ds(2 * NV, NV)], s1.at[:, 5])
    clear_pads(f, 1, 5)
    clear_pads(s1, 1, 5)
    clear_pads(s2, 1, 3)

    def first(i, row, t):
        def emit(v, h, r, s):
            rs[v, row, pl.ds(pl.multiple_of(8 * t, 8), 8), half_of(h)] = r
            s1[v, row + 1, h, pl.ds(pl.multiple_of(8 * t + 8, 8), 8), :] = s

        start_row(f, row + 1, kapb, row, nowb if later else None, prevb, row, t, jh, emit)

    groups[0].wait()
    each_tile(2, lambda i: i, first)
    groups[1].wait()
    each_tile(2, lambda i: i + 2, first)
    for i in range(2):
        c.add(rs.at[:, 3 * i], rs_out.at[:, i])
        c.halves_out(s1.at[:, 3 * i + 1], s1_out.at[:, i])

    def second(i, row, t):
        def emit(v, h, val):
            s2[v, i, h, pl.ds(pl.multiple_of(8 * t + 8, 8), 8), :] = val

        relax_row(s1, i + 1, rs, i, kapb, i, t, jh, emit)

    each_tile(4, lambda i: i, second)
    c.halves_out(s2, s2_out)

    def third(i, row, t):
        def emit(v, h, val):
            s3[v, i, pl.ds(pl.multiple_of(8 * t, 8), 8), half_of(h)] = val

        relax_row(s2, i + 1, rs, i + 1, kapb, i + 1, t, jh, emit)

    each_tile(2, lambda i: i, third)
    c.add(s3, s3_out)
    c.wait()


INNER_SCRATCH = (
    field(6), pltpu.VMEM((NV, 4, CY, CZ), F32), pltpu.VMEM((NV, 4, CY, CZ), F32), pltpu.VMEM((4, CY, CZ), F32),
    pltpu.VMEM((NV, 4, CY, CZ), F32), field(6), field(4), pltpu.VMEM((NV, 2, CY, CZ), F32), pltpu.SemaphoreType.DMA((2,)),
)


def fix_rows(rse, s1e, far, kape, jh, lo_ok, hi_ok):
    def body(i, row, t):
        y0 = pl.multiple_of(8 * t, 8)
        sign = jnp.where(i % 2 == 0, 1.0, -1.0).astype(F32)
        scale = jnp.where(i == 0, lo_ok, jnp.where(i == 3, hi_ok, 1.0))
        kp, ninv = kap_tile(kape, row + 1, t)
        for h in range(2):
            side = [far[w, i, pl.ds(y0, 8), half_of(h)] for w in range(NV)]
            turned = [side[w] * sign for w in range(NV)]
            for v in range(NV):
                r = rse[v, row + 1, pl.ds(y0, 8), half_of(h)] - kp[h] * side[v]
                for w in range(NV):
                    r = r + jh[v * 6 + w] * turned[w]
                rse[v, row + 1, pl.ds(y0, 8), half_of(h)] = r
                s1e[v, row + 2, h, pl.ds(pl.multiple_of(y0 + 8, 8), 8), :] = r * (ninv[h] * scale)

    each_tile(4, lambda i: i - 1 + 6 * (i // 2), body)


def finish_body(
    q, kap, jh, who, idx_in, pairs_in, own_lo, own_hi, got_lo, got_hi, klo, khi, w_in,
    er, rs_in, s1_in, s2_in, s3_in, qn, send,
    rse, s1e, s2e, kape, far, qb, s3, q8, tab, g, wb, idx, pairs, sem,
):
    lo_ok = jnp.where(who[1] > 0, 1.0, 0.0).astype(F32)
    hi_ok = jnp.where(who[1] < who[2] - 1, 1.0, 0.0).astype(F32)
    c, d, e, k = (Copies(sem.at[n]) for n in range(4))
    for i, msg in ((0, own_lo), (1, got_lo), (2, got_hi), (3, own_hi)):
        c.add(msg.at[pl.ds(0, NV)], far.at[:, i])
    for x, msg in ((0, got_lo), (1, own_lo), (8, own_hi), (9, got_hi)):
        c.add(msg.at[pl.ds(NV, NV)], rse.at[:, x])
    c.add(kap, kape.at[pl.ds(1, CX)])
    c.add(klo.at[3 * NV], kape.at[0])
    c.add(khi.at[3 * NV], kape.at[CX + 1])
    for x, msg in ((0, got_lo), (3, own_lo), (8, own_hi), (11, got_hi)):
        k.halves(msg.at[pl.ds(2 * NV, NV)], s1e.at[:, x])
    for i, (r, s) in enumerate(((2, 4), (7, 7))):
        k.add(er.at[:, i], rse.at[:, r])
        k.add(rs_in.at[:, i], rse.at[:, (3, 6)[i]])
        k.halves(s1_in.at[:, i], s1e.at[:, s])
    d.halves(s2_in, s2e.at[:, pl.ds(3, 4)])
    d.add(q, qb)
    d.add(s3_in, s3)
    e.add(w_in, wb)
    e.add(idx_in, idx)
    e.add(pairs_in, pairs)
    clear_pads(s1e, 1, 4)
    clear_pads(s1e, 8, 11)
    clear_pads(s2e, 1, 4)
    clear_pads(s2e, 6, 9)
    c.wait()

    fix_rows(rse, s1e, far, kape, jh, lo_ok, hi_ok)
    k.wait()

    def second(i, row, t):
        scale = jnp.where(i == 0, lo_ok, jnp.where(i == 5, hi_ok, 1.0))

        def emit(v, h, val):
            s2e[v, row + 1, h, pl.ds(pl.multiple_of(8 * t + 8, 8), 8), :] = val * scale

        relax_row(s1e, row + 2, rse, row + 1, kape, row + 1, t, jh, emit)

    each_tile(6, lambda i: i - 1 + 4 * (i // 3), second)
    d.wait()

    def put(row, v, h, t, val):
        qb[v, row, pl.ds(pl.multiple_of(8 * t, 8), 8), half_of(h)] = val
        q8[row, h, pl.ds(64 * t + v, 8, stride=8), :] = val

    def third(i, row, t):
        def emit(v, h, val):
            put(row, v, h, t, qb[v, row, pl.ds(pl.multiple_of(8 * t, 8), 8), half_of(h)] + val)

        relax_row(s2e, row + 1, rse, row + 1, kape, row + 1, t, jh, emit)

    each_tile(6, lambda i: i + 2 * (i // 3), third)

    def rest(i, row, t):
        y0 = pl.multiple_of(8 * t, 8)
        for v in range(NV):
            for h in range(2):
                put(row, v, h, t, qb[v, row, pl.ds(y0, 8), half_of(h)] + s3[v, i, pl.ds(y0, 8), half_of(h)])

    each_tile(2, lambda i: i + 3, rest)
    d.add(qb, qn)
    gather_points(idx, pairs, who[0], wb, e, send, q8, tab, g)
    d.wait()


FINISH_SCRATCH = (
    pltpu.VMEM((NV, CX + 2, CY, CZ), F32), field(CX + 4), field(CX + 2), pltpu.VMEM((CX + 2, CY, CZ), F32),
    pltpu.VMEM((NV, 4, CY, CZ), F32), pltpu.VMEM((NV, CX, CY, CZ), F32), pltpu.VMEM((NV, 2, CY, CZ), F32),
    pltpu.VMEM((CX, 2, 8 * CY, LANES), F32),
    pltpu.VMEM((DONOR_ROWS + 8, LANES), F32),
    pltpu.VMEM((2 * POINTS, LANES), F32),
    pltpu.VMEM((2, POINTS, LANES), F32),
    pltpu.SMEM((POINTS,), I32),
    pltpu.SMEM((16, 16), I32),
    pltpu.SemaphoreType.DMA((4,)),
)


def gather_points(idx, pairs, me, wb, loads, send, q8, tab, g):
    @pl.loop(0, YGROUPS)
    def _(yg):
        first = pl.multiple_of(jnp.minimum(yg * 3, CY - 4) * 8, 8)
        for xg in range(2):
            for h in range(2):
                block = [q8[xg * 3 + xx, h, pl.ds(first, 32), :] for xx in range(4)]
                row = pl.multiple_of((xg * YGROUPS + yg) * CZ + h * LANES, LANES)
                tab[pl.ds(row, LANES), :] = jnp.concatenate(block, axis=0).T

    loads.wait()

    @pl.loop(0, TILES)
    def _(tile):
        @pl.when(tile % 2 < pairs[me, tile // 2])
        def _():
            for u in range(LANES):
                row = idx[pl.multiple_of(tile * LANES, LANES) + u]
                at = pl.multiple_of(tile * 2 * LANES, 2 * LANES) + 2 * u
                g[pl.ds(at, 2), :] = tab[pl.ds(row, 2), :]

    @pl.loop(0, TILES // 8)
    def _(n):
        for u in range(8):
            o = pl.multiple_of(n * 8 * LANES + u * LANES, LANES)
            here = g[pl.ds(o * 2, LANES, stride=2), :] * wb[0, pl.ds(o, LANES), :]
            here = here + g[pl.ds(o * 2 + 1, LANES, stride=2), :] * wb[1, pl.ds(o, LANES), :]
            turned = here.T
            parts = [turned[8 * k : 8 * k + 8] for k in range(16)]
            while len(parts) > 1:
                parts = [a + b for a, b in zip(parts[::2], parts[1::2])]
            send[4 * n + u // 2, u % 2] = parts[0]


def setup_body(
    donor_in, recv_in, pairs_in, who, held_in, didx_out, ridx_out, w_out,
    donor, recv, pairs, held, didx, dpos, ridx, w, sem,
):
    c = Copies(sem.at[0])
    c.add(donor_in, donor)
    c.add(recv_in, recv)
    c.add(pairs_in, pairs)
    d = Copies(sem.at[1])
    d.add(held_in, held)
    c.wait()
    me = who[0]
    for s in range(16):
        live = pairs[s, me]
        for t in range(2):
            i = 2 * s + t
            cell = donor[s, t, 0:1, :]
            x, y, z = cell >> 13, (cell >> 8) & (CY - 1), cell & (CZ - 1)
            xg = jnp.where(x >= 3, 1, 0)
            yg = (y * 11) >> 5
            didx[i : i + 1, :] = (xg * YGROUPS + yg) * CZ + z
            dpos[i : i + 1, :] = (x - 3 * xg) * 4 + (y - jnp.minimum(yg * 3, CY - 4))
            cell = recv[s, t : t + 1, :]
            x, y, z = cell >> 13, (cell >> 8) & (CY - 1), cell & (CZ - 1)
            row = (2 * x + (y >> 4)) * CZ + z
            row = jnp.where(t < live, row, RECV_ROWS)
            ridx[i : i + 1, :] = row * 16 + (y & 15)
    c.add(didx, didx_out)
    c.add(ridx, ridx_out)
    d.wait()

    def weigh(tile, u):
        kpos = lax.broadcasted_iota(I32, (16, LANES), 0)
        base = jnp.broadcast_to(dpos[pl.ds(tile, 1), :], (16, LANES))
        o = pl.multiple_of(tile * LANES, LANES)
        for l in range(2):
            grid = jnp.zeros((16, LANES), F32)
            for i in range(2):
                for j in range(2):
                    k = 4 * i + 2 * j + l
                    row = jnp.broadcast_to(held[tile // 2, u, k : k + 1, :], (16, LANES))
                    grid = jnp.where(kpos == base + (4 * i + j), row, grid)
            wide = [jnp.broadcast_to(grid[k : k + 1], (8, LANES)) for k in range(16)]
            w[l, pl.ds(o, LANES), :] = jnp.concatenate(wide, axis=0).T

    for part in range(4):

        @pl.loop(0, TILES // 16)
        def _(m):
            for u in range(4):
                weigh(part * (TILES // 4) + 4 * m + u, u % 2)

        rows = pl.ds(part * (POINTS // 4), POINTS // 4)
        d.add(w.at[:, rows], w_out.at[:, rows])
    c.wait()
    d.wait()


SETUP_SCRATCH = (
    pltpu.VMEM((16, 2, 8, LANES), I32),
    pltpu.VMEM((16, 2, LANES), I32),
    pltpu.SMEM((16, 16), I32),
    pltpu.VMEM((16, 2, 8, LANES), F32),
    pltpu.VMEM((TILES, LANES), I32),
    pltpu.VMEM((TILES, LANES), I32),
    pltpu.VMEM((TILES, LANES), I32),
    pltpu.VMEM((2, POINTS, LANES), F32),
    pltpu.SemaphoreType.DMA((2,)),
)


def scatter_points(vals, ridx, qb, arrive, loads, write, vrep, u, ut, half=None):
    mark = lax.broadcasted_iota(I32, (8, LANES), 0) == NV
    lane = lax.broadcasted_iota(I32, (1, LANES), 1) >> 3

    @pl.loop(0, RECV_ROWS // LANES)
    def _(i):
        u[pl.ds(pl.multiple_of(i * LANES, LANES), LANES), :] = jnp.zeros((LANES, LANES), F32)

    @pl.loop(0, TILES // 8)
    def _(n):
        for k in range(8):
            v = jnp.where(mark, 1.0, vals[4 * n + k // 2, k % 2])
            rows = pl.ds(pl.multiple_of(n * 8 * LANES + k * LANES, LANES), LANES)
            vrep[rows, :] = jnp.concatenate([v] * 16, axis=0).T

    loads.wait()

    @pl.loop(0, TILES)
    def _(b):
        for j in range(LANES):
            at = pl.multiple_of(b * LANES, LANES) + j
            word = ridx[at]
            mask = (jnp.full((1, LANES), word, I32) & 15) == lane
            pltpu.store(u.at[pl.ds(word >> 4, 1), :], vrep[pl.ds(at, 1), :], mask=mask)

    @pl.loop(0, CX - 1)
    def _(x):
        for yh in range(2):
            for h in range(2):
                row = pl.multiple_of((2 * x + yh) * CZ + h * LANES, LANES)
                ut[2 * x + yh, h] = u[pl.ds(row, LANES), :].T

    arrive.wait()

    def merge(x):
        for yh in range(2):
            for h in range(2):
                for t in range(2):
                    part = ut.at[2 * x + yh, h]
                    hit = part[pl.ds(64 * t + NV, 8, stride=8), :] != 0.0
                    y = 16 * yh + 8 * t
                    for v in range(NV):
                        new = part[pl.ds(64 * t + v, 8, stride=8), :]
                        old = qb[v, x, y : y + 8, half_of(h)]
                        write(v, x, h, y, jnp.where(hit, new, old))

    pl.loop(0, 4)(merge)
    if half is not None:
        half()
    pl.loop(4, CX - 1)(merge)


def scatter_body(q, vals, ridx_in, out, qb, vrep, u, ut, ridx, sem):
    c, e = Copies(sem.at[0]), Copies(sem.at[2])
    e.add(ridx_in, ridx)
    c.add(q, qb)

    def write(v, x, h, y, val):
        qb[v, x, y : y + 8, half_of(h)] = val

    def half():
        c.add(qb.at[:, pl.ds(0, 4)], out.at[:, pl.ds(0, 4)])

    scatter_points(vals, ridx, qb, c, e, write, vrep, u, ut, half)
    c.add(qb.at[:, pl.ds(4, 4)], out.at[:, pl.ds(4, 4)])
    c.wait()


def scatter_edge_body(
    q, vals, ridx_in, now, prev, kap, jh, out, lo, hi, er,
    qb, vrep, u, ut, ridx, f, nowb, prevb, kapb, ers, es1, sem,
):
    c, e = Copies(sem.at[0]), Copies(sem.at[2])
    e.add(ridx_in, ridx)
    c.add(q, qb)
    d = Copies(sem.at[1])
    for side in range(2):
        edge_load(d, side, now, prev, kap, nowb, prevb, kapb)
    clear_pads(f, 1, 4)
    clear_pads(f, 6, 9)
    edge_zero(f)

    def write(v, x, h, y, val):
        f[v, x + 1, h, 8 + y : 16 + y, :] = val

    scatter_points(vals, ridx, qb, c, e, write, vrep, u, ut)
    for v in range(NV):
        for h in range(2):
            f[v, CX, h, 8 : 8 + CY, :] = qb[v, CX - 1, :, half_of(h)]
    c.halves_out(f.at[:, pl.ds(1, CX)], out)
    d.wait()
    for side, msg in ((0, lo), (1, hi)):
        edge_rows(side, f, kapb, nowb, prevb, jh, ers, es1)
        edge_send(d, side, f, kapb, ers, es1, msg, er)
    d.wait()
    c.wait()


STATE = (NV, CX, CY, CZ)
SCATTER_SCRATCH = (
    pltpu.VMEM((NV, CX, CY, CZ), F32),
    pltpu.VMEM((POINTS, LANES), F32),
    pltpu.VMEM((RECV_ROWS + 8, LANES), F32),
    pltpu.VMEM((RECV_GROUPS, 2, LANES, LANES), F32),
    pltpu.SMEM((POINTS,), I32),
)


def rows_of(n):
    return sds((NV, n, CY, CZ))


def shards(
    state_now, state_prev, viscosity, jacobian, donor_cell, interp_weight, recv_cell, pair_tiles
):
    now = state_now[0]
    prev = state_prev[0]
    kap = viscosity[0]
    jh = (jacobian[0] * 0.5).reshape(-1)
    count = lax.axis_size("blk")
    at = lax.axis_index("blk")
    me = lax.axis_index("comp")
    who = jnp.stack([me, at, jnp.int32(count)]).astype(I32)
    pairs = pair_tiles[0]
    forward = [(i, i + 1) for i in range(count - 1)]
    backward = [(b, a) for a, b in forward]

    def messages(planes):
        return [sds((planes, CY, CZ))] * 2 + [rows_of(2)]


    idx_shape = sds((TILES, LANES), I32)
    sems = pltpu.SemaphoreType.DMA((3,))

    lo, hi, er = call(
        edge_body, "edge", messages(3 * NV + 1), [HBM] * 3 + [SMEM], [HBM] * 3,
        scratch=(field(CX + 2),) + EDGE_SCRATCH + (sems,), cost_us=3.0,
    )(now, prev, kap, jh)
    state = now
    for sub in range(2):
        kept = HBM if sub == 0 else ANY
        got_lo = lax.ppermute(hi, "blk", forward)
        got_hi = lax.ppermute(lo, "blk", backward)
        if sub == 0:
            klo, khi = got_lo, got_hi
        inner = call(
            functools.partial(inner_body, later=sub > 0), "inner", [rows_of(n) for n in (2, 2, 4, 2)],
            [kept, HBM, HBM, HBM, SMEM, kept, kept], [kept] * 4,
            scratch=INNER_SCRATCH, vmem_mb=14, cost_us=4.0,
        )(state, now, prev, kap, jh, lo, hi)
        if sub == 0:
            weights, _ = lax.optimization_barrier((interp_weight[0, 0], lo))
            held = lax.all_to_all(weights, "comp", split_axis=0, concat_axis=0, tiled=True)
            didx, ridx, wide = call(
                setup_body, "setup", [idx_shape] * 2 + [sds((2, POINTS, LANES))],
                [HBM] * 3 + [SMEM, ANY], [HBM] * 3, scratch=SETUP_SCRATCH, cost_us=4.0,
            )(donor_cell[0, 0], recv_cell[0, 0], pairs, who, held)
            didx, ridx = didx.reshape(-1), ridx.reshape(-1)
        relaxed, send = call(
            finish_body, "finish", [sds(STATE), sds((16, 2, 8, LANES))],
            [kept, HBM, SMEM, SMEM, HBM, HBM, kept, kept, ANY, ANY, ANY, ANY, HBM] + [kept] * 5,
            [ANY, VMEM], scratch=FINISH_SCRATCH, vmem_mb=30, cost_us=14.0,
        )(
            state, kap, jh, who, didx, pairs, lo, hi, got_lo, got_hi, klo, khi, wide,
            er, *inner,
        )
        arrived = lax.all_to_all(send, "comp", split_axis=0, concat_axis=0, tiled=True)
        if sub == 0:
            state, lo, hi, er = call(
                scatter_edge_body, "scatter_edge", [sds(STATE)] + messages(3 * NV),
                [ANY, VMEM, HBM, HBM, HBM, HBM, SMEM], [ANY] * 4,
                scratch=SCATTER_SCRATCH + (field(CX + 2),) + EDGE_SCRATCH + (sems,),
                vmem_mb=20, cost_us=12.0,
            )(relaxed, arrived, ridx, now, prev, kap, jh)
        else:
            state = call(
                scatter_body, "scatter", sds(STATE), [ANY, VMEM, HBM], HBM,
                scratch=SCATTER_SCRATCH + (sems,), vmem_mb=12, cost_us=10.0,
            )(relaxed, arrived, ridx)
    return state[None]


def solution(mesh):
    in_specs = (
        P("comp", None, "blk", None, None),
        P("comp", None, "blk", None, None),
        P("comp", "blk", None, None),
        P("comp", None, None, None),
        P("comp", "blk", None, None, None, None),
        P("comp", "blk", None, None, None, None),
        P("comp", "blk", None, None, None),
        P("blk", None, None),
    )
    out_specs = P("comp", None, "blk", None, None)
    return jax.shard_map(shards, mesh=mesh, in_specs=in_specs, out_specs=out_specs, check_vma=False)
```
